32 devices in a mesh: groups: 2 (over y), frames: 16 (over z, x, core).
Axes of the slice: x: 2, y: 2, z: 4, core: 2. Of those that a mesh axis runs over, the one named last changes fastest.
Arguments:
- queries: bfloat16 [12288, 1536], P(('groups', 'frames')), parts along dimension 0, may hold values from -38 to 38
- keys: bfloat16 [12288, 1536], P(('groups', 'frames')), parts along dimension 0, may hold values from -38 to 38
- values: bfloat16 [12288, 1536], P(('groups', 'frames')), parts along dimension 0, may hold values from -6 to 6
- out_grad: bfloat16 [12288, 1536], P(('groups', 'frames')), parts along dimension 0, may hold values from -6 to 6
- tile_video: int32 [32], P('groups'), parts along dimension 0, may hold values from 0 to 1, never falling along the last dimension, each value on 1 to 12 neighbouring positions
Outputs:
- attended: bfloat16 [12288, 1536], P(('groups', 'frames')), parts along dimension 0
- grad_queries: bfloat16 [12288, 1536], P(('groups', 'frames')), parts along dimension 0
- grad_keys: bfloat16 [12288, 1536], P(('groups', 'frames')), parts along dimension 0
- grad_values: bfloat16 [12288, 1536], P(('groups', 'frames')), parts along dimension 0
The draws below stay inside these ranges and needn't reach their ends.
There are 2 independent parts, one for each index of `groups`. The reference program is written for one: setup_inputs(seed, part) draws one part's arguments, and reference() takes and returns one part's arrays. A program takes and returns all parts, laid end to end along the dimension named above; each array names one. Nothing has to cross between parts.
Inputs may be any that keep to these rules, and one draw needn't show every extreme that they name: `tile_video`: values never fall along the tiles; every video 0 to 1 holds 1 to 12 consecutive tiles.
All inputs are finite; a program needn't handle non-finite values.
Results may differ from the reference program's by a relative error of at most 0.005.
Values may be sent and summed in bfloat16 or wider, within the bound.
A program may use at most 192 MiB of HBM per device.

```python
import math
import jax
import jax.numpy as jnp
import numpy as np
from jax import lax

HEADS = 12
HEAD_DIM = 128
TILE_TOK = 384
VIDEOS = 2
TILES = 16
MOST_TILES = 12
TOKENS = 6144
D = 1536


def paired_rows(key):
    folded = jax.random.fold_in(key, 4242)
    seed_query, seed_key = jax.random.split(folded, 2)
    query_rows = jnp.clip(jax.random.normal(seed_query, (TOKENS, D), jnp.float32), -6.0, 6.0)
    key_rows = jnp.clip(jax.random.normal(seed_key, (TOKENS, D), jnp.float32), -6.0, 6.0)
    return (query_rows, key_rows)


def draw_queries(key, part):
    return paired_rows(key)[0].astype(jnp.bfloat16)


def draw_keys(key, part):
    return paired_rows(key)[1].astype(jnp.bfloat16)


def block_levels(key, shape, cuts, least, largest):
    loudness = 1.0
    for axis_at, shards_of in cuts:
        draws = jax.random.uniform(jax.random.fold_in(jax.random.fold_in(key, 6), axis_at), (shards_of,), jnp.float32, least / len(cuts), largest / len(cuts))
        loudness = loudness * jnp.repeat(jnp.exp(draws), shape[axis_at] // shards_of).reshape((-1,) + (1,) * (len(shape) - 1 - axis_at))
    return loudness


def split_up(count, total, most, lean):
    weights = [(1 << 20) // math.isqrt(grade ** lean) + 1 for grade in range(2, count + 1)]
    rest, holding = total - most - (count - 1), [1] * (count - 1)
    while rest > 0:
        candidates = [i for i in range(count - 1) if holding[i] < most]
        pool, left = sum([weights[i] for i in candidates]), rest
        for i in candidates:
            addition = min(most - holding[i], max(1, left * weights[i] // pool), rest)
            holding[i] = holding[i] + addition
            rest = rest - addition
    return np.array([most] + holding)


def ragged(stream_key, number_of, total, reach, slope):
    if number_of == 2:
        one = jax.random.randint(stream_key, (), max(1, total - reach), min(reach, total - 1) + 1)
        return jnp.stack([one, total - one])
    sizes = jnp.asarray(split_up(number_of, total, reach, slope), jnp.int32)
    couples = (number_of - 1) // 2
    giver, taker = sizes[1:1 + 2 * couples:2], sizes[2:2 + 2 * couples:2]
    room = jnp.minimum(giver - 1, reach - taker)
    shifted = jax.random.randint(jax.random.fold_in(stream_key, 1), (couples,), 0, 1 << 20) % (room + 1)
    sizes = sizes.at[1:1 + 2 * couples:2].set(giver - shifted).at[2:2 + 2 * couples:2].set(taker + shifted)
    return sizes[jax.random.permutation(jax.random.fold_in(stream_key, 2), number_of)]


def bell_draw(key, dims, scale, reach, cuts=(), kind=jnp.bfloat16):
    factor_of = block_levels(key, dims, cuts, -0.22, 0.18) if cuts else 1.0
    result = jax.random.normal(key, dims, jnp.float32) * scale * factor_of
    return jnp.minimum(jnp.maximum(result, -reach), reach).astype(kind)


def setup_inputs(seed: int = 0, part: int = 0) -> dict:
    seeds = jax.random.split(jax.random.key(seed), 6)
    own_keys = jax.random.split(jax.random.fold_in(seeds[5], part), 6)
    queries = draw_queries(jax.random.fold_in(jax.random.fold_in(seeds[5], part), 71), part)
    keys = draw_keys(jax.random.fold_in(jax.random.fold_in(seeds[5], part), 71), part)
    values = bell_draw(own_keys[2], (TOKENS, D), 1.0, 6.0, ((0, 16),))
    out_grad = bell_draw(own_keys[3], (TOKENS, D), 1.0, 6.0, ((0, 16),))
    tile_video = jnp.searchsorted(jnp.cumsum(ragged(own_keys[4], VIDEOS, TILES, MOST_TILES, 2)), jnp.arange(TILES), side="right").astype(jnp.int32)
    return dict(queries=queries, keys=keys, values=values, out_grad=out_grad, tile_video=tile_video)


def tile_pass(query_tile, key_window, value_window, grad_tile, allowed):
    score_scale = HEAD_DIM ** -0.5
    query_f = query_tile.astype(jnp.float32)
    key_f = key_window.astype(jnp.float32)
    value_f = value_window.astype(jnp.float32)
    grad_f = grad_tile.astype(jnp.float32)
    scores = jnp.einsum("qhe,khe->hqk", query_f, key_f) * score_scale
    scores = jnp.where(allowed[None, None, :], scores, -1e30)
    highest = jnp.max(scores, axis=2, keepdims=True)
    raised = jnp.exp(scores - highest)
    row_total = jnp.sum(raised, axis=2, keepdims=True)
    weights = raised / row_total
    rounded = lax.optimization_barrier(weights.astype(jnp.bfloat16)).astype(jnp.float32)
    attended = jnp.einsum("hqk,khe->qhe", rounded, value_f).astype(jnp.bfloat16)
    grad_prob = jnp.einsum("qhe,khe->hqk", grad_f, value_f)
    row_delta = jnp.sum(weights * grad_prob, axis=2, keepdims=True)
    grad_score = lax.optimization_barrier((weights * (grad_prob - row_delta)).astype(jnp.bfloat16)).astype(jnp.float32)
    grad_query = (jnp.einsum("hqk,khe->qhe", grad_score, key_f) * score_scale).astype(jnp.bfloat16)
    grad_key = jnp.einsum("hqk,qhe->khe", grad_score, query_f) * score_scale
    grad_value = jnp.einsum("hqk,qhe->khe", rounded, grad_f)
    return attended, grad_query, grad_key, grad_value


def reference(queries, keys, values, out_grad, tile_video):
    four_query = queries.reshape(TILES, TILE_TOK, HEADS, HEAD_DIM)
    four_grad = out_grad.reshape(TILES, TILE_TOK, HEADS, HEAD_DIM)
    zero_tile = jnp.zeros((1, TILE_TOK, HEADS, HEAD_DIM), keys.dtype)
    key_pad = jnp.concatenate([zero_tile, keys.reshape(TILES, TILE_TOK, HEADS, HEAD_DIM), zero_tile], axis=0)
    value_pad = jnp.concatenate([zero_tile, values.reshape(TILES, TILE_TOK, HEADS, HEAD_DIM), zero_tile], axis=0)
    outside = jnp.full((1,), -1, jnp.int32)
    video_pad = jnp.concatenate([outside, tile_video.astype(jnp.int32), outside], axis=0)
    zero_acc = jnp.zeros((TILE_TOK, HEADS, HEAD_DIM), jnp.float32)

    def tile_step(state_pair, tile_index):
        own_key, next_key, own_value, next_value = state_pair
        key_window = lax.dynamic_slice_in_dim(key_pad, tile_index, 3, 0).reshape(3 * TILE_TOK, HEADS, HEAD_DIM)
        value_window = lax.dynamic_slice_in_dim(value_pad, tile_index, 3, 0).reshape(3 * TILE_TOK, HEADS, HEAD_DIM)
        near_videos = lax.dynamic_slice_in_dim(video_pad, tile_index, 3, 0)
        own_video = lax.dynamic_index_in_dim(tile_video.astype(jnp.int32), tile_index, 0, keepdims=False)
        allowed = jnp.repeat(near_videos == own_video, TILE_TOK, total_repeat_length=3 * TILE_TOK)
        query_tile = lax.dynamic_index_in_dim(four_query, tile_index, 0, keepdims=False)
        grad_tile = lax.dynamic_index_in_dim(four_grad, tile_index, 0, keepdims=False)
        attended, grad_query, grad_key, grad_value = tile_pass(query_tile, key_window, value_window, grad_tile, allowed)
        parts_key = grad_key.reshape(3, TILE_TOK, HEADS, HEAD_DIM)
        parts_value = grad_value.reshape(3, TILE_TOK, HEADS, HEAD_DIM)
        emit_key = (own_key + parts_key[0]).astype(jnp.bfloat16)
        emit_value = (own_value + parts_value[0]).astype(jnp.bfloat16)
        new_state = (next_key + parts_key[1], parts_key[2], next_value + parts_value[1], parts_value[2])
        return new_state, (attended, grad_query, emit_key, emit_value)

    final_state, stacked = lax.scan(tile_step, (zero_acc, zero_acc, zero_acc, zero_acc), jnp.arange(TILES, dtype=jnp.int32))
    attended, grad_queries, emitted_key, emitted_value = stacked
    grad_keys = jnp.concatenate([emitted_key[1:], final_state[0].astype(jnp.bfloat16)[None]], axis=0)
    grad_values = jnp.concatenate([emitted_value[1:], final_state[2].astype(jnp.bfloat16)[None]], axis=0)
    return (attended.reshape(TOKENS, D), grad_queries.reshape(TOKENS, D),
            grad_keys.reshape(TOKENS, D), grad_values.reshape(TOKENS, D))
```

```python
import functools

import jax
import jax.numpy as jnp
from jax import lax
from jax.experimental import pallas as pl
from jax.experimental.pallas import tpu as pltpu
from jax.sharding import PartitionSpec as P

HEAD_DIM = 128
MESH = pl.DeviceIdType.MESH
LEFT, RIGHT = 0, 1
LOG2_E = 1.4426950408889634
MASKED = -1e30
AHEAD = 2


def matmul_nt(a, b):
    return lax.dot_general(a, b, (((1,), (1,)), ((), ())), preferred_element_type=jnp.float32)


def matmul_tn(a, b):
    return lax.dot_general(a, b, (((0,), (0,)), ((), ())), preferred_element_type=jnp.float32)


def matmul_nn(a, b):
    return lax.dot_general(a, b, (((1,), (0,)), ((), ())), preferred_element_type=jnp.float32)


def kernel(
    count, heads, relays, video_hbm, q_hbm, k_hbm, v_hbm, g_hbm, o_ref, dq_ref, dk_ref, dv_ref,
    own, window, partial, returned, total, passing, tile_video, video_sem,
    own_sem, kv_send, kv_recv, ret_send, ret_recv, pass_send, pass_recv,
):
    group = lax.axis_index("groups")
    me = lax.axis_index("frames")
    exists = (me > 0, me < count - 1)
    beside = (jnp.maximum(me - 1, 0), jnp.minimum(me + 1, count - 1))
    scale = HEAD_DIM ** (-0.5)
    inputs = (q_hbm, k_hbm, v_hbm, g_hbm)
    outputs = (o_ref, dq_ref, dk_ref, dv_ref)

    def columns(h):
        return pl.ds(pl.multiple_of(h * HEAD_DIM, HEAD_DIM), HEAD_DIM)

    def load(a, h):
        return pltpu.make_async_copy(inputs[a].at[:, columns(h)], own.at[a, h], own_sem.at[a, h])

    place, plane, planes = lax.rem(me, 4), me // 4, count // 4
    up = jnp.logical_and(place % 2 == 1, plane < planes - 1)
    down = jnp.logical_and(place % 2 == 0, plane > 0)
    in_relay = jnp.logical_or(up, down)
    first_peer = jnp.where(in_relay, jnp.where(place < 2, me + 2, me - 2), 0)
    second_peer = jnp.where(in_relay, jnp.where(place % 2 == 1, me + 3, me - 3), 0)

    def relayed(lower, upward, h):
        share = heads * ((planes - 1 - lower) if upward else (lower + 1)) // planes
        return (h + 1) * share // heads > h * share // heads

    is_source = (jnp.logical_and(place == 0, plane > 0), jnp.logical_and(place == 3, up))
    passes_up = jnp.logical_and(place == 1, up)
    passes_down = jnp.logical_and(place == 2, down)

    def source_of(phase, side, a, h):
        return inputs[1 + a].at[:, columns(h)] if phase == 0 else partial.at[side, a, h]

    lands = (window, returned)
    send_sems, recv_sems = (kv_send, ret_send), (kv_recv, ret_recv)

    def copy(phase, side, a, h, arrives, target):
        return pltpu.make_async_remote_copy(
            src_ref=source_of(phase, side, a, h),
            dst_ref=lands[phase].at[arrives, a, h],
            send_sem=send_sems[phase].at[side],
            recv_sem=recv_sems[phase].at[arrives, a, h],
            device_id=(group, target),
            device_id_type=MESH,
        )

    def copy_to_relay(phase, side, a, h):
        return pltpu.make_async_remote_copy(
            src_ref=source_of(phase, side, a, h),
            dst_ref=passing.at[phase, a, h],
            send_sem=send_sems[phase].at[side],
            recv_sem=pass_recv.at[phase, a, h],
            device_id=(group, first_peer),
            device_id_type=MESH,
        )

    def copy_from_relay(phase, side, a, h):
        return pltpu.make_async_remote_copy(
            src_ref=passing.at[phase, a, h],
            dst_ref=lands[phase].at[side, a, h],
            send_sem=pass_send.at[phase],
            recv_sem=recv_sems[phase].at[side, a, h],
            device_id=(group, second_peer),
            device_id_type=MESH,
        )

    def send(phase, side, h):
        lower = plane - 1 if side == LEFT else plane
        if relays:
            indirect = jnp.logical_and(is_source[side], relayed(lower, side == RIGHT, h))
            direct = jnp.logical_and(exists[side], jnp.logical_not(indirect))

            @pl.when(indirect)
            def _():
                for a in range(2):
                    copy_to_relay(phase, side, a, h).start()
        else:
            direct = exists[side]

        @pl.when(direct)
        def _():
            for a in range(2):
                copy(phase, side, a, h, 1 - side, beside[side]).start()

    def receive(phase, side, h):
        @pl.when(exists[side])
        def _():
            for a in range(2):
                copy(phase, side, a, h, side, beside[side]).wait_recv()

    def sent(phase, side):
        @pl.when(exists[side])
        def _():
            pltpu.make_async_remote_copy(
                src_ref=partial.at[side],
                dst_ref=lands[phase].at[1 - side],
                send_sem=send_sems[phase].at[side],
                recv_sem=recv_sems[phase].at[1 - side, 0, 0],
                device_id=(group, beside[side]),
                device_id_type=MESH,
            ).wait_send()

    def for_relayed(h, act):
        if relays:

            @pl.when(jnp.logical_and(passes_up, relayed(plane, True, h)))
            def _():
                act(LEFT)

            @pl.when(jnp.logical_and(passes_down, relayed(plane - 1, False, h)))
            def _():
                act(RIGHT)

    def pass_on(phase, h):
        def act(side):
            for a in range(2):
                forward = copy_from_relay(phase, side, a, h)
                copy_to_relay(phase, side, a, h).wait_recv()
                forward.start()

        for_relayed(h, act)

    def passed(phase):
        if relays:
            for lower in range(count // 4 - 1):
                for upward, side in ((True, LEFT), (False, RIGHT)):
                    share = heads * ((count // 4 - 1 - lower) if upward else (lower + 1)) // (count // 4)
                    here = (
                        jnp.logical_and(passes_up, plane == lower)
                        if upward
                        else jnp.logical_and(passes_down, plane == lower + 1)
                    )

                    @pl.when(here)
                    def _():
                        pltpu.make_async_remote_copy(
                            src_ref=passing.at[phase, :, pl.ds(0, share)],
                            dst_ref=lands[phase].at[side, :, pl.ds(0, share)],
                            send_sem=pass_send.at[phase],
                            recv_sem=recv_sems[phase].at[side, 0, 0],
                            device_id=(group, second_peer),
                            device_id_type=MESH,
                        ).wait_send()

    video_copy = pltpu.make_async_copy(video_hbm, tile_video, video_sem)
    video_copy.start()
    barrier = pltpu.get_barrier_semaphore()
    for side in (LEFT, RIGHT):

        @pl.when(exists[side])
        def _():
            pl.semaphore_signal(
                barrier, inc=1, device_id=(group, beside[side]), device_id_type=MESH
            )

    peers = jnp.minimum(me, 1) + jnp.minimum(count - 1 - me, 1)
    if relays:

        @pl.when(in_relay)
        def _():
            for peer in (first_peer, second_peer):
                pl.semaphore_signal(barrier, inc=1, device_id=(group, peer), device_id_type=MESH)

        peers = peers + jnp.where(in_relay, 2, 0)
    pl.semaphore_wait(barrier, peers)

    def start_sends(h, carry):
        for side in (LEFT, RIGHT):
            send(0, side, h)
        return carry

    def start_loads(h, carry):
        for a in range(4):
            load(a, h).start()
        return carry

    lax.fori_loop(0, heads, start_sends, 0)
    lax.fori_loop(0, heads, start_loads, 0)

    for side in (LEFT, RIGHT):

        @pl.when(jnp.logical_not(exists[side]))
        def _():
            def clear(h, carry):
                for a in range(2):
                    window[side, a, h] = jnp.zeros(window.shape[3:], window.dtype)
                    returned[side, a, h] = jnp.zeros(returned.shape[3:], returned.dtype)
                return carry

            lax.fori_loop(0, heads, clear, 0)

    video_copy.wait()
    own_video = tile_video[me]
    bias = [
        jnp.where(
            jnp.logical_and(exists[side], tile_video[beside[side]] == own_video), 0.0, MASKED
        ).astype(jnp.float32)
        for side in (LEFT, RIGHT)
    ]

    def attend(h, carry):
        for a in range(4):
            load(a, h).wait()
        pass_on(0, h)
        for side in (LEFT, RIGHT):
            receive(0, side, h)
        queries, grads = own[0, h], own[3, h]
        keys = (own[1, h], window[LEFT, 0, h], window[RIGHT, 0, h])
        values = (own[2, h], window[LEFT, 1, h], window[RIGHT, 1, h])
        scores = [matmul_nt(key, queries) * (scale * LOG2_E) for key in keys]
        scores = [scores[0], scores[1] + bias[LEFT], scores[2] + bias[RIGHT]]
        highest = functools.reduce(
            jnp.maximum, [jnp.max(s, axis=0, keepdims=True) for s in scores]
        )
        raised = [jnp.exp2(s - highest) for s in scores]
        row_total = sum(jnp.sum(r, axis=0, keepdims=True) for r in raised)
        inverse = 1.0 / row_total
        weights = [r * inverse for r in raised]
        rounded = [w.astype(jnp.bfloat16) for w in weights]
        grad_prob = [matmul_nt(value, grads) for value in values]
        row_delta = sum(
            jnp.sum(w * p, axis=0, keepdims=True) for w, p in zip(weights, grad_prob)
        )
        grad_score = [
            (w * (p - row_delta)).astype(jnp.bfloat16) for w, p in zip(weights, grad_prob)
        ]
        for place, side in ((1, LEFT), (2, RIGHT)):
            partial[side, 0, h] = (matmul_nn(grad_score[place], queries) * scale).astype(
                jnp.bfloat16
            )
            partial[side, 1, h] = matmul_nn(rounded[place], grads).astype(jnp.bfloat16)
            send(1, side, h)
        total[0, h] = matmul_nn(grad_score[0], queries) * scale
        total[1, h] = matmul_nn(rounded[0], grads)
        attended = sum(matmul_tn(v, r) for v, r in zip(values, rounded))
        grad_query = sum(matmul_tn(k, s) for k, s in zip(keys, grad_score)) * scale
        outputs[0][:, columns(h)] = attended.T.astype(jnp.bfloat16)
        outputs[1][:, columns(h)] = grad_query.T.astype(jnp.bfloat16)
        return carry

    lax.fori_loop(0, heads, attend, 0)

    def pass_first(h, carry):
        pass_on(1, h)
        return carry

    lax.fori_loop(0, min(AHEAD, heads), pass_first, 0)

    def finish(h, carry):
        @pl.when(h + AHEAD < heads)
        def _():
            pass_on(1, h + AHEAD)

        for side in (LEFT, RIGHT):
            receive(1, side, h)
        for a in range(2):
            joined = (
                total[a, h]
                + returned[LEFT, a, h].astype(jnp.float32)
                + returned[RIGHT, a, h].astype(jnp.float32)
            )
            outputs[2 + a][:, columns(h)] = joined.astype(jnp.bfloat16)
        return carry

    lax.fori_loop(0, heads, finish, 0)

    for phase in (0, 1):
        for side in (LEFT, RIGHT):
            sent(phase, side)
        passed(phase)


def place_kernel(*refs):
    sources, targets, sem = refs[:4], refs[4:8], refs[8]
    copies = [
        pltpu.make_async_copy(source, target, sem.at[i])
        for i, (source, target) in enumerate(zip(sources, targets))
    ]
    for copy in copies:
        copy.start()
    for copy in copies:
        copy.wait()


def two_wide(mesh):
    spots = [
        (tuple(d.coords), d.core_on_chip) if hasattr(d, "coords") else None
        for d in mesh.devices.reshape(mesh.devices.shape[0], -1)[0]
    ]
    if len(spots) < 8 or len(spots) % 4 or None in spots:
        return False
    (x0, _, z0), _ = spots[0]
    return all(
        coords[0] - x0 == i // 2 % 2 and coords[2] - z0 == i // 4 and core == i % 2
        for i, (coords, core) in enumerate(spots)
    )


def solution(mesh):
    count = mesh.shape["frames"]
    relays = two_wide(mesh)

    def step(queries, keys, values, out_grad, tile_video):
        rows, width = queries.shape
        heads = width // HEAD_DIM
        tile = (heads, rows, HEAD_DIM)
        results = pl.pallas_call(
            functools.partial(kernel, count, heads, relays),
            out_shape=[jax.ShapeDtypeStruct((rows, width), jnp.bfloat16)] * 4,
            in_specs=[pl.BlockSpec(memory_space=pltpu.HBM)] * 5,
            out_specs=[pl.BlockSpec(memory_space=pltpu.VMEM)] * 4,
            scratch_shapes=[
                pltpu.VMEM((4,) + tile, jnp.bfloat16),
                pltpu.VMEM((2, 2) + tile, jnp.bfloat16),
                pltpu.VMEM((2, 2) + tile, jnp.bfloat16),
                pltpu.VMEM((2, 2) + tile, jnp.bfloat16),
                pltpu.VMEM((2,) + tile, jnp.float32),
                pltpu.VMEM((2, 2) + tile, jnp.bfloat16),
                pltpu.SMEM(tile_video.shape, tile_video.dtype),
                pltpu.SemaphoreType.DMA,
                pltpu.SemaphoreType.DMA((4, heads)),
                pltpu.SemaphoreType.DMA((2,)),
                pltpu.SemaphoreType.DMA((2, 2, heads)),
                pltpu.SemaphoreType.DMA((2,)),
                pltpu.SemaphoreType.DMA((2, 2, heads)),
                pltpu.SemaphoreType.DMA((2,)),
                pltpu.SemaphoreType.DMA((2, 2, heads)),
            ],
            compiler_params=pltpu.CompilerParams(
                collective_id=0, has_side_effects=True, vmem_limit_bytes=49 * 1024 * 1024
            ),
        )(tile_video, queries, keys, values, out_grad)
        return pl.pallas_call(
            place_kernel,
            out_shape=[jax.ShapeDtypeStruct((rows, width), jnp.bfloat16)] * 4,
            in_specs=[pl.BlockSpec(memory_space=pltpu.VMEM)] * 4,
            out_specs=[pl.BlockSpec(memory_space=pltpu.HBM)] * 4,
            scratch_shapes=[pltpu.SemaphoreType.DMA((4,))],
            compiler_params=pltpu.CompilerParams(vmem_limit_bytes=8 * 1024 * 1024),
        )(*results)

    rows = P(("groups", "frames"), None)
    return jax.shard_map(
        step,
        mesh=mesh,
        in_specs=(rows, rows, rows, rows, P("groups")),
        out_specs=(rows, rows, rows, rows),
        check_vma=False,
    )
```

```python
import functools

import jax
import jax.numpy as jnp
from jax import lax
from jax.experimental import pallas as pl
from jax.experimental.pallas import tpu as pltpu
from jax.sharding import PartitionSpec as P

HEAD_DIM = 128
MESH = pl.DeviceIdType.MESH
LEFT, RIGHT = 0, 1
LOG2_E = 1.4426950408889634
MASKED = -1e30
AHEAD = 2


def matmul_nt(a, b):
    return lax.dot_general(a, b, (((1,), (1,)), ((), ())), preferred_element_type=jnp.float32)


def matmul_tn(a, b):
    return lax.dot_general(a, b, (((0,), (0,)), ((), ())), preferred_element_type=jnp.float32)


def matmul_nn(a, b):
    return lax.dot_general(a, b, (((1,), (0,)), ((), ())), preferred_element_type=jnp.float32)


def kernel(
    count, heads, relays, video_hbm, q_hbm, k_hbm, v_hbm, g_hbm, o_ref, dq_ref, dk_ref, dv_ref,
    own, window, partial, returned, total, passing, tile_video, video_sem,
    own_sem, kv_send, kv_recv, ret_send, ret_recv, pass_send, pass_recv,
):
    group = lax.axis_index("groups")
    me = lax.axis_index("frames")
    exists = (me > 0, me < count - 1)
    beside = (jnp.maximum(me - 1, 0), jnp.minimum(me + 1, count - 1))
    scale = HEAD_DIM ** (-0.5)
    inputs = (q_hbm, k_hbm, v_hbm, g_hbm)
    outputs = (o_ref, dq_ref, dk_ref, dv_ref)

    def columns(h):
        return pl.ds(pl.multiple_of(h * HEAD_DIM, HEAD_DIM), HEAD_DIM)

    def load(a, h):
        return pltpu.make_async_copy(inputs[a].at[:, columns(h)], own.at[a, h], own_sem)

    place, plane, planes = lax.rem(me, 4), me // 4, count // 4
    up = jnp.logical_and(place % 2 == 1, plane < planes - 1)
    down = jnp.logical_and(place % 2 == 0, plane > 0)
    in_relay = jnp.logical_or(up, down)
    first_peer = jnp.where(in_relay, jnp.where(place < 2, me + 2, me - 2), 0)
    second_peer = jnp.where(in_relay, jnp.where(place % 2 == 1, me + 3, me - 3), 0)

    def relayed(lower, upward, h):
        share = heads * ((planes - 1 - lower) if upward else (lower + 1)) // planes
        return (h + 1) * share // heads > h * share // heads

    is_source = (jnp.logical_and(place == 0, plane > 0), jnp.logical_and(place == 3, up))
    passes_up = jnp.logical_and(place == 1, up)
    passes_down = jnp.logical_and(place == 2, down)

    lands = (window, returned)
    send_sems, recv_sems = (kv_send, ret_send), (kv_recv, ret_recv)

    def pieces(phase, side, h):
        if phase == 1:
            return [(partial.at[side, :, h], slice(None))]
        return [(inputs[1 + a].at[:, columns(h)], a) for a in range(2)]

    def direct_copies(phase, side, h):
        return [
            pltpu.make_async_remote_copy(
                src_ref=source,
                dst_ref=lands[phase].at[1 - side, a, h],
                send_sem=send_sems[phase].at[side],
                recv_sem=recv_sems[phase].at[h],
                device_id=(group, beside[side]),
                device_id_type=MESH,
            )
            for source, a in pieces(phase, side, h)
        ]

    def copies_to_relay(phase, side, h):
        return [
            pltpu.make_async_remote_copy(
                src_ref=source,
                dst_ref=passing.at[phase, a, h],
                send_sem=send_sems[phase].at[side],
                recv_sem=pass_recv.at[phase, h],
                device_id=(group, first_peer),
                device_id_type=MESH,
            )
            for source, a in pieces(phase, side, h)
        ]

    def copy_from_relay(phase, side, h):
        return pltpu.make_async_remote_copy(
            src_ref=passing.at[phase, :, h],
            dst_ref=lands[phase].at[side, :, h],
            send_sem=pass_send.at[phase],
            recv_sem=recv_sems[phase].at[h],
            device_id=(group, second_peer),
            device_id_type=MESH,
        )

    def send(phase, side, h):
        lower = plane - 1 if side == LEFT else plane
        if relays:
            indirect = jnp.logical_and(is_source[side], relayed(lower, side == RIGHT, h))
            direct = jnp.logical_and(exists[side], jnp.logical_not(indirect))

            @pl.when(indirect)
            def _():
                for copy in copies_to_relay(phase, side, h):
                    copy.start()
        else:
            direct = exists[side]

        @pl.when(direct)
        def _():
            for copy in direct_copies(phase, side, h):
                copy.start()

    def arrived(buffer, sem):
        pltpu.make_async_copy(buffer, buffer, sem).wait()

    def receive(phase, h):
        for left in (True, False):
            for right in (True, False):
                if not (left or right):
                    continue
                sides = slice(None) if left and right else (LEFT if left else RIGHT)

                @pl.when(jnp.logical_and(exists[LEFT] == left, exists[RIGHT] == right))
                def _():
                    arrived(lands[phase].at[sides, :, h], recv_sems[phase].at[h])

    def sent(phase, side):
        @pl.when(exists[side])
        def _():
            pltpu.make_async_remote_copy(
                src_ref=partial.at[side],
                dst_ref=lands[phase].at[1 - side],
                send_sem=send_sems[phase].at[side],
                recv_sem=recv_sems[phase].at[0],
                device_id=(group, beside[side]),
                device_id_type=MESH,
            ).wait_send()

    def for_relayed(h, act):
        if relays:

            @pl.when(jnp.logical_and(passes_up, relayed(plane, True, h)))
            def _():
                act(LEFT)

            @pl.when(jnp.logical_and(passes_down, relayed(plane - 1, False, h)))
            def _():
                act(RIGHT)

    def pass_on(phase, h):
        def act(side):
            arrived(passing.at[phase, :, h], pass_recv.at[phase, h])
            copy_from_relay(phase, side, h).start()

        for_relayed(h, act)

    def passed(phase):
        if relays:
            for lower in range(count // 4 - 1):
                for upward, side in ((True, LEFT), (False, RIGHT)):
                    share = heads * ((count // 4 - 1 - lower) if upward else (lower + 1)) // (count // 4)
                    here = (
                        jnp.logical_and(passes_up, plane == lower)
                        if upward
                        else jnp.logical_and(passes_down, plane == lower + 1)
                    )

                    @pl.when(here)
                    def _():
                        pltpu.make_async_remote_copy(
                            src_ref=passing.at[phase, :, pl.ds(0, share)],
                            dst_ref=lands[phase].at[side, :, pl.ds(0, share)],
                            send_sem=pass_send.at[phase],
                            recv_sem=recv_sems[phase].at[0],
                            device_id=(group, second_peer),
                            device_id_type=MESH,
                        ).wait_send()

    video_copy = pltpu.make_async_copy(video_hbm, tile_video, video_sem)
    video_copy.start()
    barrier = pltpu.get_barrier_semaphore()
    for side in (LEFT, RIGHT):

        @pl.when(exists[side])
        def _():
            pl.semaphore_signal(
                barrier, inc=1, device_id=(group, beside[side]), device_id_type=MESH
            )

    peers = jnp.minimum(me, 1) + jnp.minimum(count - 1 - me, 1)
    if relays:

        @pl.when(in_relay)
        def _():
            for peer in (first_peer, second_peer):
                pl.semaphore_signal(barrier, inc=1, device_id=(group, peer), device_id_type=MESH)

        peers = peers + jnp.where(in_relay, 2, 0)
    pl.semaphore_wait(barrier, peers)

    def start_sends(crossing):
        def act(h, carry):
            for side in (LEFT, RIGHT):

                @pl.when((lax.rem(me, 2) == 1) == ((side == RIGHT) == crossing))
                def _():
                    send(0, side, h)

            return carry

        return act

    def start_loads(h, carry):
        for a in range(4):
            load(a, h).start()
        return carry

    for crossing in (True, False):
        lax.fori_loop(0, heads, start_sends(crossing), 0)
    lax.fori_loop(0, heads, start_loads, 0)

    for side in (LEFT, RIGHT):

        @pl.when(jnp.logical_not(exists[side]))
        def _():
            def clear(h, carry):
                for a in range(2):
                    window[side, a, h] = jnp.zeros(window.shape[3:], window.dtype)
                    returned[side, a, h] = jnp.zeros(returned.shape[3:], returned.dtype)
                return carry

            lax.fori_loop(0, heads, clear, 0)

    video_copy.wait()
    arrived(own, own_sem)
    own_video = tile_video[me]
    bias = [
        jnp.where(
            jnp.logical_and(exists[side], tile_video[beside[side]] == own_video), 0.0, MASKED
        ).astype(jnp.float32)
        for side in (LEFT, RIGHT)
    ]

    def attend(h, carry):
        pass_on(0, h)
        receive(0, h)
        queries, grads = own[0, h], own[3, h]
        keys = (own[1, h], window[LEFT, 0, h], window[RIGHT, 0, h])
        values = (own[2, h], window[LEFT, 1, h], window[RIGHT, 1, h])
        scores = [matmul_nt(key, queries) * (scale * LOG2_E) for key in keys]
        scores = [scores[0], scores[1] + bias[LEFT], scores[2] + bias[RIGHT]]
        highest = functools.reduce(
            jnp.maximum, [jnp.max(s, axis=0, keepdims=True) for s in scores]
        )
        raised = [jnp.exp2(s - highest) for s in scores]
        row_total = sum(jnp.sum(r, axis=0, keepdims=True) for r in raised)
        inverse = 1.0 / row_total
        weights = [r * inverse for r in raised]
        rounded = [w.astype(jnp.bfloat16) for w in weights]
        grad_prob = [matmul_nt(value, grads) for value in values]
        row_delta = sum(
            jnp.sum(w * p, axis=0, keepdims=True) for w, p in zip(weights, grad_prob)
        )
        grad_score = [
            (w * (p - row_delta)).astype(jnp.bfloat16) for w, p in zip(weights, grad_prob)
        ]
        for place, side in ((1, LEFT), (2, RIGHT)):
            partial[side, 0, h] = (matmul_nn(grad_score[place], queries) * scale).astype(
                jnp.bfloat16
            )
            partial[side, 1, h] = matmul_nn(rounded[place], grads).astype(jnp.bfloat16)
            send(1, side, h)
        total[0, h] = matmul_nn(grad_score[0], queries) * scale
        total[1, h] = matmul_nn(rounded[0], grads)
        attended = sum(matmul_tn(v, r) for v, r in zip(values, rounded))
        grad_query = sum(matmul_tn(k, s) for k, s in zip(keys, grad_score)) * scale
        outputs[0][:, columns(h)] = attended.T.astype(jnp.bfloat16)
        outputs[1][:, columns(h)] = grad_query.T.astype(jnp.bfloat16)
        return carry

    lax.fori_loop(0, heads, attend, 0)

    def pass_first(h, carry):
        pass_on(1, h)
        return carry

    lax.fori_loop(0, min(AHEAD, heads), pass_first, 0)

    def finish(h, carry):
        @pl.when(h + AHEAD < heads)
        def _():
            pass_on(1, h + AHEAD)

        receive(1, h)
        for a in range(2):
            joined = (
                total[a, h]
                + returned[LEFT, a, h].astype(jnp.float32)
                + returned[RIGHT, a, h].astype(jnp.float32)
            )
            outputs[2 + a][:, columns(h)] = joined.astype(jnp.bfloat16)
        return carry

    lax.fori_loop(0, heads, finish, 0)

    for phase in (0, 1):
        for side in (LEFT, RIGHT):
            sent(phase, side)
        passed(phase)


def place_kernel(*refs):
    sources, targets, sem = refs[:4], refs[4:8], refs[8]
    copies = [
        pltpu.make_async_copy(source, target, sem.at[i])
        for i, (source, target) in enumerate(zip(sources, targets))
    ]
    for copy in copies:
        copy.start()
    for copy in copies:
        copy.wait()


def two_wide(mesh):
    spots = [
        (tuple(d.coords), d.core_on_chip) if hasattr(d, "coords") else None
        for d in mesh.devices.reshape(mesh.devices.shape[0], -1)[0]
    ]
    if len(spots) < 8 or len(spots) % 4 or None in spots:
        return False
    (x0, _, z0), _ = spots[0]
    return all(
        coords[0] - x0 == i // 2 % 2 and coords[2] - z0 == i // 4 and core == i % 2
        for i, (coords, core) in enumerate(spots)
    )


def solution(mesh):
    count = mesh.shape["frames"]
    relays = two_wide(mesh)

    def step(queries, keys, values, out_grad, tile_video):
        rows, width = queries.shape
        heads = width // HEAD_DIM
        tile = (heads, rows, HEAD_DIM)
        results = pl.pallas_call(
            functools.partial(kernel, count, heads, relays),
            out_shape=[jax.ShapeDtypeStruct((rows, width), jnp.bfloat16)] * 4,
            in_specs=[pl.BlockSpec(memory_space=pltpu.HBM)] * 5,
            out_specs=[pl.BlockSpec(memory_space=pltpu.VMEM)] * 4,
            scratch_shapes=[
                pltpu.VMEM((4,) + tile, jnp.bfloat16),
                pltpu.VMEM((2, 2) + tile, jnp.bfloat16),
                pltpu.VMEM((2, 2) + tile, jnp.bfloat16),
                pltpu.VMEM((2, 2) + tile, jnp.bfloat16),
                pltpu.VMEM((2,) + tile, jnp.float32),
                pltpu.VMEM((2, 2) + tile, jnp.bfloat16),
                pltpu.SMEM(tile_video.shape, tile_video.dtype),
                pltpu.SemaphoreType.DMA,
                pltpu.SemaphoreType.DMA,
                pltpu.SemaphoreType.DMA((2,)),
                pltpu.SemaphoreType.DMA((heads,)),
                pltpu.SemaphoreType.DMA((2,)),
                pltpu.SemaphoreType.DMA((heads,)),
                pltpu.SemaphoreType.DMA((2,)),
                pltpu.SemaphoreType.DMA((2, heads)),
            ],
            compiler_params=pltpu.CompilerParams(
                collective_id=0, has_side_effects=True, vmem_limit_bytes=49 * 1024 * 1024
            ),
        )(pltpu.with_memory_space_constraint(tile_video, pltpu.HBM), queries, keys, values, out_grad)
        return pl.pallas_call(
            place_kernel,
            out_shape=[jax.ShapeDtypeStruct((rows, width), jnp.bfloat16)] * 4,
            in_specs=[pl.BlockSpec(memory_space=pltpu.VMEM)] * 4,
            out_specs=[pl.BlockSpec(memory_space=pltpu.HBM)] * 4,
            scratch_shapes=[pltpu.SemaphoreType.DMA((4,))],
            compiler_params=pltpu.CompilerParams(vmem_limit_bytes=8 * 1024 * 1024),
        )(*results)

    rows = P(("groups", "frames"), None)
    return jax.shard_map(
        step,
        mesh=mesh,
        in_specs=(rows, rows, rows, rows, P("groups")),
        out_specs=(rows, rows, rows, rows),
        check_vma=False,
    )
```

```python
import functools

import jax
import jax.numpy as jnp
from jax import lax
from jax.experimental import pallas as pl
from jax.experimental.pallas import tpu as pltpu
from jax.sharding import PartitionSpec as P

HEAD_DIM = 128
MESH = pl.DeviceIdType.MESH
LEFT, RIGHT = 0, 1
LOG2_E = 1.4426950408889634
MASKED = -1e30
AHEAD = 3
BATCH = 3


def matmul_nt(a, b):
    return lax.dot_general(a, b, (((1,), (1,)), ((), ())), preferred_element_type=jnp.float32)


def matmul_tn(a, b):
    return lax.dot_general(a, b, (((0,), (0,)), ((), ())), preferred_element_type=jnp.float32)


def matmul_nn(a, b):
    return lax.dot_general(a, b, (((1,), (0,)), ((), ())), preferred_element_type=jnp.float32)


def batches_of(heads):
    even = range(0, heads, BATCH)
    arrivals = (even, sorted({0, heads // 2, heads * 3 // 4, heads - 1}))
    passes = (even, even)
    return [
        [
            [(first, last - first) for first, last in zip(firsts, list(firsts[1:]) + [heads])]
            for firsts in cut
        ]
        for cut in (arrivals, passes)
    ]


def kernel(
    count, heads, relays, video_hbm, q_hbm, k_hbm, v_hbm, g_hbm, o_ref, dq_ref, dk_ref, dv_ref,
    own, window, partial, returned, total, passing, tile_video, video_sem,
    own_sem, kv_send, kv_recv, ret_send, ret_recv, pass_send, pass_recv, ready,
):
    group = lax.axis_index("groups")
    me = lax.axis_index("frames")
    exists = (me > 0, me < count - 1)
    beside = (jnp.maximum(me - 1, 0), jnp.minimum(me + 1, count - 1))
    scale = HEAD_DIM ** (-0.5)
    inputs = (q_hbm, k_hbm, v_hbm, g_hbm)
    outputs = (o_ref, dq_ref, dk_ref, dv_ref)

    def columns(h):
        return pl.ds(pl.multiple_of(h * HEAD_DIM, HEAD_DIM), HEAD_DIM)

    def load(a, h):
        return pltpu.make_async_copy(inputs[a].at[:, columns(h)], own.at[a, h], own_sem)

    place, plane, planes = lax.rem(me, 4), me // 4, count // 4
    batches, passings = batches_of(heads)
    up = jnp.logical_and(place % 2 == 1, plane < planes - 1)
    down = jnp.logical_and(place % 2 == 0, plane > 0)
    in_relay = jnp.logical_or(up, down)
    first_peer = jnp.where(in_relay, jnp.where(place < 2, me + 2, me - 2), 0)
    second_peer = jnp.where(in_relay, jnp.where(place % 2 == 1, me + 3, me - 3), 0)

    def share_of(lower, upward):
        return heads * ((planes - 1 - lower) if upward else (lower + 1)) // planes

    def picked(share, h):
        return (heads - h) * share // heads > (heads - 1 - h) * share // heads

    def batch_of(cut, h):
        return sum(jnp.where(h >= first, 1, 0) for first, _ in cut[1:])

    is_source = (jnp.logical_and(place == 0, plane > 0), jnp.logical_and(place == 3, up))
    passes_up = jnp.logical_and(place == 1, up)
    passes_down = jnp.logical_and(place == 2, down)

    lands = (window, returned)
    send_sems, recv_sems = (kv_send, ret_send), (kv_recv, ret_recv)

    def pieces(phase, side, h):
        if phase == 1:
            return [(partial.at[side, :, h], slice(None))]
        return [(inputs[1 + a].at[:, columns(h)], a) for a in range(2)]

    def direct_copies(phase, side, h):
        return [
            pltpu.make_async_remote_copy(
                src_ref=source,
                dst_ref=lands[phase].at[1 - side, a, h],
                send_sem=send_sems[phase].at[side],
                recv_sem=recv_sems[phase].at[batch_of(batches[phase], h)],
                device_id=(group, beside[side]),
                device_id_type=MESH,
            )
            for source, a in pieces(phase, side, h)
        ]

    def copies_to_relay(phase, side, h):
        return [
            pltpu.make_async_remote_copy(
                src_ref=source,
                dst_ref=passing.at[phase, a, h],
                send_sem=send_sems[phase].at[side],
                recv_sem=pass_recv.at[phase, batch_of(passings[phase], h)],
                device_id=(group, first_peer),
                device_id_type=MESH,
            )
            for source, a in pieces(phase, side, h)
        ]

    def copy_from_relay(phase, side, h):
        return pltpu.make_async_remote_copy(
            src_ref=passing.at[phase, :, h],
            dst_ref=lands[phase].at[side, :, h],
            send_sem=pass_send.at[phase],
            recv_sem=recv_sems[phase].at[batch_of(batches[phase], h)],
            device_id=(group, second_peer),
            device_id_type=MESH,
        )

    def send(phase, side, h):
        lower = plane - 1 if side == LEFT else plane
        if relays:
            indirect = jnp.logical_and(is_source[side], picked(share_of(lower, side == RIGHT), h))
            direct = jnp.logical_and(exists[side], jnp.logical_not(indirect))

            @pl.when(indirect)
            def _():
                for copy in copies_to_relay(phase, side, h):
                    copy.start()
        else:
            direct = exists[side]

        @pl.when(direct)
        def _():
            for copy in direct_copies(phase, side, h):
                copy.start()

    def arrived(buffer, sem):
        pltpu.make_async_copy(buffer, buffer, sem).wait()

    def receive(phase, batch):
        first, size = batches[phase][batch]
        for left in (True, False):
            for right in (True, False):
                if not (left or right):
                    continue
                sides = slice(None) if left and right else (LEFT if left else RIGHT)

                @pl.when(jnp.logical_and(exists[LEFT] == left, exists[RIGHT] == right))
                def _():
                    arrived(
                        lands[phase].at[sides, :, pl.ds(first, size)], recv_sems[phase].at[batch]
                    )

    def sent(phase, side):
        @pl.when(exists[side])
        def _():
            pltpu.make_async_remote_copy(
                src_ref=partial.at[side],
                dst_ref=lands[phase].at[1 - side],
                send_sem=send_sems[phase].at[side],
                recv_sem=recv_sems[phase].at[0],
                device_id=(group, beside[side]),
                device_id_type=MESH,
            ).wait_send()

    def passers():
        for lower in range(planes - 1 if relays else 0):
            yield jnp.logical_and(passes_up, plane == lower), LEFT, share_of(lower, True)
            yield jnp.logical_and(passes_down, plane == lower + 1), RIGHT, share_of(lower, False)

    def pass_on(phase, batch):
        first, size = passings[phase][batch]
        for here, side, share in passers():
            through = [h for h in range(first, first + size) if picked(share, h)]
            if not through:
                continue

            @pl.when(here)
            def _():
                arrived(
                    passing.at[phase, :, pl.ds(first, len(through))], pass_recv.at[phase, batch]
                )
                for h in through:
                    copy_from_relay(phase, side, h).start()

    def pass_at(phase, h):
        for batch, (first, _) in enumerate(passings[phase]):

            @pl.when(h == first)
            def _():
                pass_on(phase, batch)

    def receive_at(phase, h):
        for batch, (first, _) in enumerate(batches[phase]):

            @pl.when(h == first)
            def _():
                receive(phase, batch)

    def passed(phase):
        for here, side, share in passers():

            @pl.when(here)
            def _():
                pltpu.make_async_remote_copy(
                    src_ref=passing.at[phase, :, pl.ds(0, share)],
                    dst_ref=lands[phase].at[side, :, pl.ds(0, share)],
                    send_sem=pass_send.at[phase],
                    recv_sem=recv_sems[phase].at[0],
                    device_id=(group, second_peer),
                    device_id_type=MESH,
                ).wait_send()

    video_copy = pltpu.make_async_copy(video_hbm, tile_video, video_sem)
    video_copy.start()
    barrier = pltpu.get_barrier_semaphore()
    for side in (LEFT, RIGHT):

        @pl.when(exists[side])
        def _():
            pl.semaphore_signal(
                barrier, inc=1, device_id=(group, beside[side]), device_id_type=MESH
            )

    peers = jnp.minimum(me, 1) + jnp.minimum(count - 1 - me, 1)
    if relays:
        passes = jnp.logical_or(passes_up, passes_down)
        uses = jnp.logical_and(in_relay, jnp.logical_not(passes))

        @pl.when(passes)
        def _():
            for peer in (first_peer, second_peer):
                pl.semaphore_signal(barrier, inc=1, device_id=(group, peer), device_id_type=MESH)

        peers = peers + jnp.where(uses, 2, 0)
    pl.semaphore_wait(barrier, peers)

    def start_sends(crossing):
        def act(h, carry):
            for side in (LEFT, RIGHT):

                @pl.when((lax.rem(me, 2) == 1) == ((side == RIGHT) == crossing))
                def _():
                    send(0, side, h)

            return carry

        return act

    def start_loads(h, carry):
        for a in range(4):
            load(a, h).start()
        return carry

    early = min(AHEAD, heads)
    lax.fori_loop(0, heads, start_sends(True), 0)
    lax.fori_loop(0, early, start_sends(False), 0)
    if relays:

        @pl.when(uses)
        def _():
            pl.semaphore_signal(
                ready, inc=1, device_id=(group, second_peer), device_id_type=MESH
            )

    lax.fori_loop(0, heads, start_loads, 0)

    for side in (LEFT, RIGHT):

        @pl.when(jnp.logical_not(exists[side]))
        def _():
            def clear(h, carry):
                for a in range(2):
                    window[side, a, h] = jnp.zeros(window.shape[3:], window.dtype)
                    returned[side, a, h] = jnp.zeros(returned.shape[3:], returned.dtype)
                return carry

            lax.fori_loop(0, heads, clear, 0)

    video_copy.wait()
    arrived(own, own_sem)
    own_video = tile_video[me]
    bias = [
        jnp.where(
            jnp.logical_and(exists[side], tile_video[beside[side]] == own_video), 0.0, MASKED
        ).astype(jnp.float32)
        for side in (LEFT, RIGHT)
    ]

    if relays:

        @pl.when(passes)
        def _():
            pl.semaphore_wait(ready, 1)

    def attend(h, carry):
        pass_at(0, h)
        receive_at(0, h)

        @pl.when(h + early < heads)
        def _():
            start_sends(False)(h + early, 0)

        queries, grads = own[0, h], own[3, h]
        keys = (own[1, h], window[LEFT, 0, h], window[RIGHT, 0, h])
        values = (own[2, h], window[LEFT, 1, h], window[RIGHT, 1, h])
        scores = [matmul_nt(key, queries) * (scale * LOG2_E) for key in keys]
        scores = [scores[0], scores[1] + bias[LEFT], scores[2] + bias[RIGHT]]
        highest = functools.reduce(
            jnp.maximum, [jnp.max(s, axis=0, keepdims=True) for s in scores]
        )
        raised = [jnp.exp2(s - highest) for s in scores]
        row_total = sum(jnp.sum(r, axis=0, keepdims=True) for r in raised)
        inverse = 1.0 / row_total
        weights = [r * inverse for r in raised]
        rounded = [w.astype(jnp.bfloat16) for w in weights]
        grad_prob = [matmul_nt(value, grads) for value in values]
        row_delta = sum(
            jnp.sum(w * p, axis=0, keepdims=True) for w, p in zip(weights, grad_prob)
        )
        grad_score = [
            (w * (p - row_delta)).astype(jnp.bfloat16) for w, p in zip(weights, grad_prob)
        ]
        for place, side in ((1, LEFT), (2, RIGHT)):
            partial[side, 0, h] = (matmul_nn(grad_score[place], queries) * scale).astype(
                jnp.bfloat16
            )
            partial[side, 1, h] = matmul_nn(rounded[place], grads).astype(jnp.bfloat16)
            send(1, side, h)
        total[0, h] = matmul_nn(grad_score[0], queries) * scale
        total[1, h] = matmul_nn(rounded[0], grads)
        attended = sum(matmul_tn(v, r) for v, r in zip(values, rounded))
        grad_query = sum(matmul_tn(k, s) for k, s in zip(keys, grad_score)) * scale
        outputs[0][:, columns(h)] = attended.T.astype(jnp.bfloat16)
        outputs[1][:, columns(h)] = grad_query.T.astype(jnp.bfloat16)
        return carry

    lax.fori_loop(0, heads, attend, 0)

    def drain(phase):
        for side in (LEFT, RIGHT):
            sent(phase, side)
        passed(phase)

    drain(0)

    for batch, (first, _) in enumerate(passings[1]):
        if first < AHEAD:
            pass_on(1, batch)

    def finish(h, carry):
        pass_at(1, h + AHEAD)
        receive_at(1, h)
        for a in range(2):
            joined = (
                total[a, h]
                + returned[LEFT, a, h].astype(jnp.float32)
                + returned[RIGHT, a, h].astype(jnp.float32)
            )
            outputs[2 + a][:, columns(h)] = joined.astype(jnp.bfloat16)
        return carry

    lax.fori_loop(0, heads, finish, 0)

    drain(1)


def place_kernel(*refs):
    sources, targets, sem = refs[:4], refs[4:8], refs[8]
    copies = [
        pltpu.make_async_copy(source, target, sem.at[i])
        for i, (source, target) in enumerate(zip(sources, targets))
    ]
    for copy in copies:
        copy.start()
    for copy in copies:
        copy.wait()


def two_wide(mesh):
    spots = [
        (tuple(d.coords), d.core_on_chip) if hasattr(d, "coords") else None
        for d in mesh.devices.reshape(mesh.devices.shape[0], -1)[0]
    ]
    if len(spots) < 8 or len(spots) % 4 or None in spots:
        return False
    (x0, _, z0), _ = spots[0]
    return all(
        coords[0] - x0 == i // 2 % 2 and coords[2] - z0 == i // 4 and core == i % 2
        for i, (coords, core) in enumerate(spots)
    )


def solution(mesh):
    count = mesh.shape["frames"]
    relays = two_wide(mesh)

    def step(queries, keys, values, out_grad, tile_video):
        rows, width = queries.shape
        heads = width // HEAD_DIM
        tile = (heads, rows, HEAD_DIM)
        waits, passes = ([len(cut) for cut in cuts] for cuts in batches_of(heads))
        results = pl.pallas_call(
            functools.partial(kernel, count, heads, relays),
            out_shape=[jax.ShapeDtypeStruct((rows, width), jnp.bfloat16)] * 4,
            in_specs=[pl.BlockSpec(memory_space=pltpu.HBM)] * 5,
            out_specs=[pl.BlockSpec(memory_space=pltpu.VMEM)] * 4,
            scratch_shapes=[
                pltpu.VMEM((4,) + tile, jnp.bfloat16),
                pltpu.VMEM((2, 2) + tile, jnp.bfloat16),
                pltpu.VMEM((2, 2) + tile, jnp.bfloat16),
                pltpu.VMEM((2, 2) + tile, jnp.bfloat16),
                pltpu.VMEM((2,) + tile, jnp.float32),
                pltpu.VMEM((2, 2) + tile, jnp.bfloat16),
                pltpu.SMEM(tile_video.shape, tile_video.dtype),
                pltpu.SemaphoreType.DMA,
                pltpu.SemaphoreType.DMA,
                pltpu.SemaphoreType.DMA((2,)),
                pltpu.SemaphoreType.DMA((waits[0],)),
                pltpu.SemaphoreType.DMA((2,)),
                pltpu.SemaphoreType.DMA((waits[1],)),
                pltpu.SemaphoreType.DMA((2,)),
                pltpu.SemaphoreType.DMA((2, max(passes))),
                pltpu.SemaphoreType.REGULAR,
            ],
            compiler_params=pltpu.CompilerParams(
                collective_id=0, has_side_effects=True, vmem_limit_bytes=49 * 1024 * 1024
            ),
        )(pltpu.with_memory_space_constraint(tile_video, pltpu.HBM), queries, keys, values, out_grad)
        return pl.pallas_call(
            place_kernel,
            out_shape=[jax.ShapeDtypeStruct((rows, width), jnp.bfloat16)] * 4,
            in_specs=[pl.BlockSpec(memory_space=pltpu.VMEM)] * 4,
            out_specs=[pl.BlockSpec(memory_space=pltpu.HBM)] * 4,
            scratch_shapes=[pltpu.SemaphoreType.DMA((4,))],
            compiler_params=pltpu.CompilerParams(vmem_limit_bytes=8 * 1024 * 1024),
        )(*results)

    rows = P(("groups", "frames"), None)
    return jax.shard_map(
        step,
        mesh=mesh,
        in_specs=(rows, rows, rows, rows, P("groups")),
        out_specs=(rows, rows, rows, rows),
        check_vma=False,
    )
```

```python
import functools

import jax
import jax.numpy as jnp
from jax import lax
from jax.experimental import pallas as pl
from jax.experimental.pallas import tpu as pltpu
from jax.sharding import PartitionSpec as P

HEAD_DIM = 128
MESH = pl.DeviceIdType.MESH
LEFT, RIGHT = 0, 1
LOG2_E = 1.4426950408889634
MASKED = -1e30
AHEAD = 3
BATCH = 3


def matmul_nt(a, b):
    return lax.dot_general(a, b, (((1,), (1,)), ((), ())), preferred_element_type=jnp.float32)


def matmul_tn(a, b):
    return lax.dot_general(a, b, (((0,), (0,)), ((), ())), preferred_element_type=jnp.float32)


def matmul_nn(a, b):
    return lax.dot_general(a, b, (((1,), (0,)), ((), ())), preferred_element_type=jnp.float32)


def batches_of(heads):
    even = range(0, heads, BATCH)
    arrivals = (even, sorted({0, heads // 2, heads * 3 // 4, heads - 1}))
    passes = (even, even)
    return [
        [
            [(first, last - first) for first, last in zip(firsts, list(firsts[1:]) + [heads])]
            for firsts in cut
        ]
        for cut in (arrivals, passes)
    ]


def kernel(
    count, heads, relays, video_hbm, q_hbm, k_hbm, v_hbm, g_hbm, o_ref, dq_ref, dk_ref, dv_ref,
    own, window, partial, returned, total, passing, tile_video, video_sem,
    own_sem, kv_send, kv_recv, ret_send, ret_recv, pass_send, pass_recv, part_sem, ready,
):
    group = lax.axis_index("groups")
    me = lax.axis_index("frames")
    exists = (me > 0, me < count - 1)
    beside = (jnp.maximum(me - 1, 0), jnp.minimum(me + 1, count - 1))
    scale = HEAD_DIM ** (-0.5)
    inputs = (q_hbm, k_hbm, v_hbm, g_hbm)
    outputs = (o_ref, dq_ref, dk_ref, dv_ref)

    def columns(h):
        return pl.ds(pl.multiple_of(h * HEAD_DIM, HEAD_DIM), HEAD_DIM)

    def load(a, h):
        return pltpu.make_async_copy(inputs[a].at[:, columns(h)], own.at[a, h], own_sem)

    place, plane, planes = lax.rem(me, 4), me // 4, count // 4
    batches, passings = batches_of(heads)
    up = jnp.logical_and(place % 2 == 1, plane < planes - 1)
    down = jnp.logical_and(place % 2 == 0, plane > 0)
    in_relay = jnp.logical_or(up, down)
    first_peer = jnp.where(in_relay, jnp.where(place < 2, me + 2, me - 2), 0)
    second_peer = jnp.where(in_relay, jnp.where(place % 2 == 1, me + 3, me - 3), 0)

    def share_of(lower, upward):
        return heads * ((planes - 1 - lower) if upward else (lower + 1)) // planes

    def picked(share, h):
        return (heads - h) * share // heads > (heads - 1 - h) * share // heads

    def rows_of(lower):
        return own.shape[2] * (lower + 1) // planes // 16 * 16

    def batch_of(cut, h):
        return sum(jnp.where(h >= first, 1, 0) for first, _ in cut[1:])

    is_source = (jnp.logical_and(place == 0, plane > 0), jnp.logical_and(place == 3, up))
    passes_up = jnp.logical_and(place == 1, up)
    passes_down = jnp.logical_and(place == 2, down)

    lands = (window, returned)
    send_sems, recv_sems = (kv_send, ret_send), (kv_recv, ret_recv)

    def pieces(phase, side, h):
        if phase == 1:
            return [(partial.at[side, :, h], slice(None))]
        return [(inputs[1 + a].at[:, columns(h)], a) for a in range(2)]

    def direct_copies(phase, side, h):
        return [
            pltpu.make_async_remote_copy(
                src_ref=source,
                dst_ref=lands[phase].at[1 - side, a, h],
                send_sem=send_sems[phase].at[side],
                recv_sem=recv_sems[phase].at[batch_of(batches[phase], h)],
                device_id=(group, beside[side]),
                device_id_type=MESH,
            )
            for source, a in pieces(phase, side, h)
        ]

    def copies_to_relay(phase, side, h, most=2):
        return [
            pltpu.make_async_remote_copy(
                src_ref=source,
                dst_ref=passing.at[phase, a, h],
                send_sem=send_sems[phase].at[side],
                recv_sem=pass_recv.at[phase, batch_of(passings[phase], h)],
                device_id=(group, first_peer),
                device_id_type=MESH,
            )
            for source, a in pieces(phase, side, h)[:most]
        ]

    def copy_from_relay(phase, side, h):
        return pltpu.make_async_remote_copy(
            src_ref=passing.at[phase, :, h],
            dst_ref=lands[phase].at[side, :, h],
            send_sem=pass_send.at[phase],
            recv_sem=recv_sems[phase].at[batch_of(batches[phase], h)],
            device_id=(group, second_peer),
            device_id_type=MESH,
        )

    def values_to_relay(lower):
        near = pl.ds(0, rows_of(lower))
        far = pl.ds(rows_of(lower), own.shape[2] - rows_of(lower))
        return [
            pltpu.make_async_remote_copy(
                src_ref=inputs[2].at[near, columns(0)],
                dst_ref=passing.at[0, 1, 0, near],
                send_sem=kv_send.at[RIGHT],
                recv_sem=part_sem.at[0],
                device_id=(group, first_peer),
                device_id_type=MESH,
            ),
            pltpu.make_async_remote_copy(
                src_ref=inputs[2].at[far, columns(0)],
                dst_ref=window.at[LEFT, 1, 0, far],
                send_sem=kv_send.at[RIGHT],
                recv_sem=kv_recv.at[0],
                device_id=(group, beside[RIGHT]),
                device_id_type=MESH,
            ),
        ]

    def parts_from_relay(lower):
        near = pl.ds(0, rows_of(lower))
        return [
            pltpu.make_async_remote_copy(
                src_ref=source,
                dst_ref=target,
                send_sem=part_sem.at[1 + i],
                recv_sem=kv_recv.at[0],
                device_id=(group, second_peer),
                device_id_type=MESH,
            )
            for i, (source, target) in enumerate(
                [
                    (passing.at[0, 0, 0], window.at[LEFT, 0, 0]),
                    (passing.at[0, 1, 0, near], window.at[LEFT, 1, 0, near]),
                ]
            )
        ]

    def send(phase, side, h):
        lower = plane - 1 if side == LEFT else plane
        if relays:
            indirect = jnp.logical_and(is_source[side], picked(share_of(lower, side == RIGHT), h))
            direct = jnp.logical_and(exists[side], jnp.logical_not(indirect))

            parted = phase == 0 and side == RIGHT
            whole = jnp.logical_and(indirect, h > 0) if parted else indirect

            @pl.when(whole)
            def _():
                for copy in copies_to_relay(phase, side, h):
                    copy.start()

            for low in range(planes - 1 if parted else 0):

                @pl.when(jnp.logical_and(indirect, jnp.logical_and(h == 0, plane == low)))
                def _():
                    for copy in copies_to_relay(0, RIGHT, 0, 1) + values_to_relay(low):
                        copy.start()
        else:
            direct = exists[side]

        @pl.when(direct)
        def _():
            for copy in direct_copies(phase, side, h):
                copy.start()

    def arrived(buffer, sem):
        pltpu.make_async_copy(buffer, buffer, sem).wait()

    def receive(phase, batch):
        first, size = batches[phase][batch]
        for left in (True, False):
            for right in (True, False):
                if not (left or right):
                    continue
                sides = slice(None) if left and right else (LEFT if left else RIGHT)

                @pl.when(jnp.logical_and(exists[LEFT] == left, exists[RIGHT] == right))
                def _():
                    arrived(
                        lands[phase].at[sides, :, pl.ds(first, size)], recv_sems[phase].at[batch]
                    )

    def sent(phase, side):
        @pl.when(exists[side])
        def _():
            pltpu.make_async_remote_copy(
                src_ref=partial.at[side],
                dst_ref=lands[phase].at[1 - side],
                send_sem=send_sems[phase].at[side],
                recv_sem=recv_sems[phase].at[0],
                device_id=(group, beside[side]),
                device_id_type=MESH,
            ).wait_send()

    def passers():
        for lower in range(planes - 1 if relays else 0):
            yield lower, jnp.logical_and(passes_up, plane == lower), LEFT
            yield lower, jnp.logical_and(passes_down, plane == lower + 1), RIGHT

    def pass_on(phase, batch):
        first, size = passings[phase][batch]
        for lower, here, side in passers():
            share = share_of(lower, side == LEFT)
            through = [h for h in range(first, first + size) if picked(share, h)]
            if not through:
                continue
            parted = phase == 0 and side == LEFT and first == 0
            tiles = (0, pl.ds(0, 2 * len(through) - 1))
            due = tiles if parted else (slice(None), pl.ds(first, len(through)))

            @pl.when(here)
            def _():
                arrived(passing.at[(phase, *due)], pass_recv.at[phase, batch])
                if parted:
                    arrived(passing.at[0, 1, 0, pl.ds(0, rows_of(lower))], part_sem.at[0])
                    for copy in parts_from_relay(lower):
                        copy.start()
                for h in through[1:] if parted else through:
                    copy_from_relay(phase, side, h).start()

    def pass_at(phase, h):
        for batch, (first, _) in enumerate(passings[phase]):

            @pl.when(h == first)
            def _():
                pass_on(phase, batch)

    def receive_at(phase, h):
        for batch, (first, _) in enumerate(batches[phase]):

            @pl.when(h == first)
            def _():
                receive(phase, batch)

    def passed(phase):
        for lower, here, side in passers():
            parted = phase == 0 and side == LEFT
            share = share_of(lower, side == LEFT) - (1 if parted else 0)

            @pl.when(here)
            def _():
                if parted:
                    for copy in parts_from_relay(lower):
                        copy.wait_send()
                if share:
                    pltpu.make_async_remote_copy(
                        src_ref=passing.at[phase, :, pl.ds(0, share)],
                        dst_ref=lands[phase].at[side, :, pl.ds(0, share)],
                        send_sem=pass_send.at[phase],
                        recv_sem=recv_sems[phase].at[0],
                        device_id=(group, second_peer),
                        device_id_type=MESH,
                    ).wait_send()

    video_copy = pltpu.make_async_copy(video_hbm, tile_video, video_sem)
    video_copy.start()
    barrier = pltpu.get_barrier_semaphore()
    for side in (LEFT, RIGHT):

        @pl.when(exists[side])
        def _():
            pl.semaphore_signal(
                barrier, inc=1, device_id=(group, beside[side]), device_id_type=MESH
            )

    peers = jnp.minimum(me, 1) + jnp.minimum(count - 1 - me, 1)
    if relays:
        passes = jnp.logical_or(passes_up, passes_down)
        uses = jnp.logical_and(in_relay, jnp.logical_not(passes))

        @pl.when(passes)
        def _():
            for peer in (first_peer, second_peer):
                pl.semaphore_signal(barrier, inc=1, device_id=(group, peer), device_id_type=MESH)

        peers = peers + jnp.where(uses, 2, 0)
    pl.semaphore_wait(barrier, peers)

    def start_sends(crossing):
        def act(h, carry):
            for side in (LEFT, RIGHT):

                @pl.when((lax.rem(me, 2) == 1) == ((side == RIGHT) == crossing))
                def _():
                    send(0, side, h)

            return carry

        return act

    def start_loads(h, carry):
        for a in range(4):
            load(a, h).start()
        return carry

    early = min(AHEAD, heads)
    lax.fori_loop(0, heads, start_sends(True), 0)
    lax.fori_loop(0, early, start_sends(False), 0)
    if relays:

        @pl.when(uses)
        def _():
            pl.semaphore_signal(
                ready, inc=1, device_id=(group, second_peer), device_id_type=MESH
            )

    lax.fori_loop(0, heads, start_loads, 0)

    for side in (LEFT, RIGHT):

        @pl.when(jnp.logical_not(exists[side]))
        def _():
            def clear(h, carry):
                for a in range(2):
                    window[side, a, h] = jnp.zeros(window.shape[3:], window.dtype)
                    returned[side, a, h] = jnp.zeros(returned.shape[3:], returned.dtype)
                return carry

            lax.fori_loop(0, heads, clear, 0)

    video_copy.wait()
    arrived(own, own_sem)
    own_video = tile_video[me]
    bias = [
        jnp.where(
            jnp.logical_and(exists[side], tile_video[beside[side]] == own_video), 0.0, MASKED
        ).astype(jnp.float32)
        for side in (LEFT, RIGHT)
    ]

    if relays:

        @pl.when(passes)
        def _():
            pl.semaphore_wait(ready, 1)

    def attend(h, carry):
        pass_at(0, h)
        receive_at(0, h)

        @pl.when(h + early < heads)
        def _():
            start_sends(False)(h + early, 0)

        queries, grads = own[0, h], own[3, h]
        keys = (own[1, h], window[LEFT, 0, h], window[RIGHT, 0, h])
        values = (own[2, h], window[LEFT, 1, h], window[RIGHT, 1, h])
        scores = [matmul_nt(key, queries) * (scale * LOG2_E) for key in keys]
        scores = [scores[0], scores[1] + bias[LEFT], scores[2] + bias[RIGHT]]
        highest = functools.reduce(
            jnp.maximum, [jnp.max(s, axis=0, keepdims=True) for s in scores]
        )
        raised = [jnp.exp2(s - highest) for s in scores]
        row_total = sum(jnp.sum(r, axis=0, keepdims=True) for r in raised)
        inverse = 1.0 / row_total
        weights = [r * inverse for r in raised]
        rounded = [w.astype(jnp.bfloat16) for w in weights]
        grad_prob = [matmul_nt(value, grads) for value in values]
        row_delta = sum(
            jnp.sum(w * p, axis=0, keepdims=True) for w, p in zip(weights, grad_prob)
        )
        grad_score = [
            (w * (p - row_delta)).astype(jnp.bfloat16) for w, p in zip(weights, grad_prob)
        ]
        for place, side in ((1, LEFT), (2, RIGHT)):
            partial[side, 0, h] = (matmul_nn(grad_score[place], queries) * scale).astype(
                jnp.bfloat16
            )
            partial[side, 1, h] = matmul_nn(rounded[place], grads).astype(jnp.bfloat16)
            send(1, side, h)
        total[0, h] = matmul_nn(grad_score[0], queries) * scale
        total[1, h] = matmul_nn(rounded[0], grads)
        attended = sum(matmul_tn(v, r) for v, r in zip(values, rounded))
        grad_query = sum(matmul_tn(k, s) for k, s in zip(keys, grad_score)) * scale
        outputs[0][:, columns(h)] = attended.T.astype(jnp.bfloat16)
        outputs[1][:, columns(h)] = grad_query.T.astype(jnp.bfloat16)
        return carry

    lax.fori_loop(0, heads, attend, 0)

    def drain(phase):
        for side in (LEFT, RIGHT):
            sent(phase, side)
        passed(phase)

    drain(0)

    for batch, (first, _) in enumerate(passings[1]):
        if first < AHEAD:
            pass_on(1, batch)

    def finish(h, carry):
        pass_at(1, h + AHEAD)
        receive_at(1, h)
        for a in range(2):
            joined = (
                total[a, h]
                + returned[LEFT, a, h].astype(jnp.float32)
                + returned[RIGHT, a, h].astype(jnp.float32)
            )
            outputs[2 + a][:, columns(h)] = joined.astype(jnp.bfloat16)
        return carry

    lax.fori_loop(0, heads, finish, 0)

    drain(1)


def place_kernel(*refs):
    sources, targets, sem = refs[:4], refs[4:8], refs[8]
    copies = [
        pltpu.make_async_copy(source, target, sem.at[i])
        for i, (source, target) in enumerate(zip(sources, targets))
    ]
    for copy in copies:
        copy.start()
    for copy in copies:
        copy.wait()


def two_wide(mesh):
    spots = [
        (tuple(d.coords), d.core_on_chip) if hasattr(d, "coords") else None
        for d in mesh.devices.reshape(mesh.devices.shape[0], -1)[0]
    ]
    if len(spots) < 8 or len(spots) % 4 or None in spots:
        return False
    (x0, _, z0), _ = spots[0]
    return all(
        coords[0] - x0 == i // 2 % 2 and coords[2] - z0 == i // 4 and core == i % 2
        for i, (coords, core) in enumerate(spots)
    )


def solution(mesh):
    count = mesh.shape["frames"]
    relays = two_wide(mesh)

    def step(queries, keys, values, out_grad, tile_video):
        rows, width = queries.shape
        heads = width // HEAD_DIM
        tile = (heads, rows, HEAD_DIM)
        waits, passes = ([len(cut) for cut in cuts] for cuts in batches_of(heads))
        results = pl.pallas_call(
            functools.partial(kernel, count, heads, relays),
            out_shape=[jax.ShapeDtypeStruct((rows, width), jnp.bfloat16)] * 4,
            in_specs=[pl.BlockSpec(memory_space=pltpu.HBM)] * 5,
            out_specs=[pl.BlockSpec(memory_space=pltpu.VMEM)] * 4,
            scratch_shapes=[
                pltpu.VMEM((4,) + tile, jnp.bfloat16),
                pltpu.VMEM((2, 2) + tile, jnp.bfloat16),
                pltpu.VMEM((2, 2) + tile, jnp.bfloat16),
                pltpu.VMEM((2, 2) + tile, jnp.bfloat16),
                pltpu.VMEM((2,) + tile, jnp.float32),
                pltpu.VMEM((2, 2) + tile, jnp.bfloat16),
                pltpu.SMEM(tile_video.shape, tile_video.dtype),
                pltpu.SemaphoreType.DMA,
                pltpu.SemaphoreType.DMA,
                pltpu.SemaphoreType.DMA((2,)),
                pltpu.SemaphoreType.DMA((waits[0],)),
                pltpu.SemaphoreType.DMA((2,)),
                pltpu.SemaphoreType.DMA((waits[1],)),
                pltpu.SemaphoreType.DMA((2,)),
                pltpu.SemaphoreType.DMA((2, max(passes))),
                pltpu.SemaphoreType.DMA((3,)),
                pltpu.SemaphoreType.REGULAR,
            ],
            compiler_params=pltpu.CompilerParams(
                collective_id=0, has_side_effects=True, vmem_limit_bytes=49 * 1024 * 1024
            ),
        )(pltpu.with_memory_space_constraint(tile_video, pltpu.HBM), queries, keys, values, out_grad)
        return pl.pallas_call(
            place_kernel,
            out_shape=[jax.ShapeDtypeStruct((rows, width), jnp.bfloat16)] * 4,
            in_specs=[pl.BlockSpec(memory_space=pltpu.VMEM)] * 4,
            out_specs=[pl.BlockSpec(memory_space=pltpu.HBM)] * 4,
            scratch_shapes=[pltpu.SemaphoreType.DMA((4,))],
            compiler_params=pltpu.CompilerParams(vmem_limit_bytes=8 * 1024 * 1024),
        )(*results)

    rows = P(("groups", "frames"), None)
    return jax.shard_map(
        step,
        mesh=mesh,
        in_specs=(rows, rows, rows, rows, P("groups")),
        out_specs=(rows, rows, rows, rows),
        check_vma=False,
    )
```

```python
import functools

import jax
import jax.numpy as jnp
from jax import lax
from jax.experimental import pallas as pl
from jax.experimental.pallas import tpu as pltpu
from jax.sharding import PartitionSpec as P

HEAD_DIM = 128
MESH = pl.DeviceIdType.MESH
LEFT, RIGHT = 0, 1
LOG2_E = 1.4426950408889634
MASKED = -1e30
AHEAD = 3
BATCH = 3


def matmul_nt(a, b):
    return lax.dot_general(a, b, (((1,), (1,)), ((), ())), preferred_element_type=jnp.float32)


def matmul_tn(a, b):
    return lax.dot_general(a, b, (((0,), (0,)), ((), ())), preferred_element_type=jnp.float32)


def matmul_nn(a, b):
    return lax.dot_general(a, b, (((1,), (0,)), ((), ())), preferred_element_type=jnp.float32)


def batches_of(heads):
    even = range(0, heads, BATCH)
    arrivals = (even, sorted({0, heads // 2, heads * 3 // 4, heads - 1}))
    passes = (even, even)
    return [
        [
            [(first, last - first) for first, last in zip(firsts, list(firsts[1:]) + [heads])]
            for firsts in cut
        ]
        for cut in (arrivals, passes)
    ]


def kernel(
    count, heads, relays, video_hbm, q_hbm, k_hbm, v_hbm, g_hbm, o_ref, dq_ref, dk_ref, dv_ref,
    own, window, partial, returned, total, passing, tile_video, video_sem,
    own_sem, kv_send, kv_recv, ret_send, ret_recv, pass_send, pass_recv, part_sem, ready,
):
    group = lax.axis_index("groups")
    me = lax.axis_index("frames")
    exists = (me > 0, me < count - 1)
    beside = (jnp.maximum(me - 1, 0), jnp.minimum(me + 1, count - 1))
    scale = HEAD_DIM ** (-0.5)
    inputs = (q_hbm, k_hbm, v_hbm, g_hbm)
    outputs = (o_ref, dq_ref, dk_ref, dv_ref)

    def columns(h):
        return pl.ds(pl.multiple_of(h * HEAD_DIM, HEAD_DIM), HEAD_DIM)

    def load(a, h):
        return pltpu.make_async_copy(inputs[a].at[:, columns(h)], own.at[a, h], own_sem)

    place, plane, planes = lax.rem(me, 4), me // 4, count // 4
    batches, passings = batches_of(heads)
    up = jnp.logical_and(place % 2 == 1, plane < planes - 1)
    down = jnp.logical_and(place % 2 == 0, plane > 0)
    in_relay = jnp.logical_or(up, down)
    first_peer = jnp.where(in_relay, jnp.where(place < 2, me + 2, me - 2), 0)
    second_peer = jnp.where(in_relay, jnp.where(place % 2 == 1, me + 3, me - 3), 0)

    def share_of(lower, upward):
        return heads * ((planes - 1 - lower) if upward else (lower + 1)) // planes

    def picked(share, h):
        return (heads - h) * share // heads > (heads - 1 - h) * share // heads

    def rows_of(lower):
        return own.shape[2] * (lower + 1) // planes // 16 * 16

    def batch_of(cut, h):
        return sum(jnp.where(h >= first, 1, 0) for first, _ in cut[1:])

    is_source = (jnp.logical_and(place == 0, plane > 0), jnp.logical_and(place == 3, up))
    passes_up = jnp.logical_and(place == 1, up)
    passes_down = jnp.logical_and(place == 2, down)

    lands = (window, returned)
    send_sems, recv_sems = (kv_send, ret_send), (kv_recv, ret_recv)

    def pieces(phase, side, h):
        if phase == 1:
            return [(partial.at[side, :, h], slice(None))]
        return [(inputs[1 + a].at[:, columns(h)], a) for a in range(2)]

    def direct_copies(phase, side, h):
        return [
            pltpu.make_async_remote_copy(
                src_ref=source,
                dst_ref=lands[phase].at[1 - side, a, h],
                send_sem=send_sems[phase].at[side],
                recv_sem=recv_sems[phase].at[batch_of(batches[phase], h)],
                device_id=(group, beside[side]),
                device_id_type=MESH,
            )
            for source, a in pieces(phase, side, h)
        ]

    def copies_to_relay(phase, side, h, most=2):
        return [
            pltpu.make_async_remote_copy(
                src_ref=source,
                dst_ref=passing.at[phase, a, h],
                send_sem=send_sems[phase].at[side],
                recv_sem=pass_recv.at[phase, batch_of(passings[phase], h)],
                device_id=(group, first_peer),
                device_id_type=MESH,
            )
            for source, a in pieces(phase, side, h)[:most]
        ]

    def copy_from_relay(phase, side, h):
        return pltpu.make_async_remote_copy(
            src_ref=passing.at[phase, :, h],
            dst_ref=lands[phase].at[side, :, h],
            send_sem=pass_send.at[phase],
            recv_sem=recv_sems[phase].at[batch_of(batches[phase], h)],
            device_id=(group, second_peer),
            device_id_type=MESH,
        )

    def values_to_relay(lower):
        near = pl.ds(0, rows_of(lower))
        far = pl.ds(rows_of(lower), own.shape[2] - rows_of(lower))
        return [
            pltpu.make_async_remote_copy(
                src_ref=inputs[2].at[near, columns(0)],
                dst_ref=passing.at[0, 1, 0, near],
                send_sem=kv_send.at[RIGHT],
                recv_sem=part_sem.at[0],
                device_id=(group, first_peer),
                device_id_type=MESH,
            ),
            pltpu.make_async_remote_copy(
                src_ref=inputs[2].at[far, columns(0)],
                dst_ref=window.at[LEFT, 1, 0, far],
                send_sem=kv_send.at[RIGHT],
                recv_sem=kv_recv.at[0],
                device_id=(group, beside[RIGHT]),
                device_id_type=MESH,
            ),
        ]

    def parts_from_relay(lower):
        near = pl.ds(0, rows_of(lower))
        return [
            pltpu.make_async_remote_copy(
                src_ref=source,
                dst_ref=target,
                send_sem=part_sem.at[1 + i],
                recv_sem=kv_recv.at[0],
                device_id=(group, second_peer),
                device_id_type=MESH,
            )
            for i, (source, target) in enumerate(
                [
                    (passing.at[0, 0, 0], window.at[LEFT, 0, 0]),
                    (passing.at[0, 1, 0, near], window.at[LEFT, 1, 0, near]),
                ]
            )
        ]

    def send(phase, side, h):
        lower = plane - 1 if side == LEFT else plane
        if relays:
            indirect = jnp.logical_and(is_source[side], picked(share_of(lower, side == RIGHT), h))
            direct = jnp.logical_and(exists[side], jnp.logical_not(indirect))

            parted = phase == 0 and side == RIGHT
            whole = jnp.logical_and(indirect, h > 0) if parted else indirect

            @pl.when(whole)
            def _():
                for copy in copies_to_relay(phase, side, h):
                    copy.start()

            for low in range(planes - 1 if parted else 0):

                @pl.when(jnp.logical_and(indirect, jnp.logical_and(h == 0, plane == low)))
                def _():
                    for copy in copies_to_relay(0, RIGHT, 0, 1) + values_to_relay(low):
                        copy.start()
        else:
            direct = exists[side]

        @pl.when(direct)
        def _():
            for copy in direct_copies(phase, side, h):
                copy.start()

    def arrived(buffer, sem):
        pltpu.make_async_copy(buffer, buffer, sem).wait()

    def receive(phase, batch):
        first, size = batches[phase][batch]
        for left in (True, False):
            for right in (True, False):
                if not (left or right):
                    continue
                sides = slice(None) if left and right else (LEFT if left else RIGHT)

                @pl.when(jnp.logical_and(exists[LEFT] == left, exists[RIGHT] == right))
                def _():
                    arrived(
                        lands[phase].at[sides, :, pl.ds(first, size)], recv_sems[phase].at[batch]
                    )

    def sent(phase, side):
        @pl.when(exists[side])
        def _():
            pltpu.make_async_remote_copy(
                src_ref=partial.at[side],
                dst_ref=lands[phase].at[1 - side],
                send_sem=send_sems[phase].at[side],
                recv_sem=recv_sems[phase].at[0],
                device_id=(group, beside[side]),
                device_id_type=MESH,
            ).wait_send()

    def passers():
        for lower in range(planes - 1 if relays else 0):
            yield lower, jnp.logical_and(passes_up, plane == lower), LEFT
            yield lower, jnp.logical_and(passes_down, plane == lower + 1), RIGHT

    def pass_on(phase, batch):
        first, size = passings[phase][batch]
        for lower, here, side in passers():
            share = share_of(lower, side == LEFT)
            through = [h for h in range(first, first + size) if picked(share, h)]
            if not through:
                continue
            parted = phase == 0 and side == LEFT and first == 0
            tiles = (0, pl.ds(0, 2 * len(through) - 1))
            due = tiles if parted else (slice(None), pl.ds(first, len(through)))

            @pl.when(here)
            def _():
                arrived(passing.at[(phase, *due)], pass_recv.at[phase, batch])
                if parted:
                    arrived(passing.at[0, 1, 0, pl.ds(0, rows_of(lower))], part_sem.at[0])
                    for copy in parts_from_relay(lower):
                        copy.start()
                for h in through[1:] if parted else through:
                    copy_from_relay(phase, side, h).start()

    def pass_at(phase, h):
        for batch, (first, _) in enumerate(passings[phase]):

            @pl.when(h == first)
            def _():
                pass_on(phase, batch)

    def receive_at(phase, h):
        for batch, (first, _) in enumerate(batches[phase]):

            @pl.when(h == first)
            def _():
                receive(phase, batch)

    def passed(phase):
        for lower, here, side in passers():
            parted = phase == 0 and side == LEFT
            share = share_of(lower, side == LEFT) - (1 if parted else 0)

            @pl.when(here)
            def _():
                if parted:
                    for copy in parts_from_relay(lower):
                        copy.wait_send()
                if share:
                    pltpu.make_async_remote_copy(
                        src_ref=passing.at[phase, :, pl.ds(0, share)],
                        dst_ref=lands[phase].at[side, :, pl.ds(0, share)],
                        send_sem=pass_send.at[phase],
                        recv_sem=recv_sems[phase].at[0],
                        device_id=(group, second_peer),
                        device_id_type=MESH,
                    ).wait_send()

    barrier = pltpu.get_barrier_semaphore()
    for side in (LEFT, RIGHT):

        @pl.when(exists[side])
        def _():
            pl.semaphore_signal(
                barrier, inc=1, device_id=(group, beside[side]), device_id_type=MESH
            )

    peers = jnp.minimum(me, 1) + jnp.minimum(count - 1 - me, 1)
    if relays:
        passes = jnp.logical_or(passes_up, passes_down)
        uses = jnp.logical_and(in_relay, jnp.logical_not(passes))

        @pl.when(passes)
        def _():
            for peer in (first_peer, second_peer):
                pl.semaphore_signal(barrier, inc=1, device_id=(group, peer), device_id_type=MESH)

        peers = peers + jnp.where(uses, 2, 0)
    pl.semaphore_wait(barrier, peers)

    def start_sends(crossing):
        def act(h, carry):
            for side in (LEFT, RIGHT):

                @pl.when((lax.rem(me, 2) == 1) == ((side == RIGHT) == crossing))
                def _():
                    send(0, side, h)

            return carry

        return act

    def start_loads(h, carry):
        for a in range(4):
            load(a, h).start()
        return carry

    early = min(AHEAD, heads)
    lax.fori_loop(0, heads, start_sends(True), 0)
    lax.fori_loop(0, early, start_sends(False), 0)
    if relays:

        @pl.when(uses)
        def _():
            pl.semaphore_signal(
                ready, inc=1, device_id=(group, second_peer), device_id_type=MESH
            )

    video_copy = pltpu.make_async_copy(video_hbm, tile_video, video_sem)
    video_copy.start()
    lax.fori_loop(0, heads, start_loads, 0)

    for side in (LEFT, RIGHT):

        @pl.when(jnp.logical_not(exists[side]))
        def _():
            def clear(h, carry):
                for a in range(2):
                    window[side, a, h] = jnp.zeros(window.shape[3:], window.dtype)
                    returned[side, a, h] = jnp.zeros(returned.shape[3:], returned.dtype)
                return carry

            lax.fori_loop(0, heads, clear, 0)

    video_copy.wait()
    arrived(own, own_sem)
    own_video = tile_video[me]
    bias = [
        jnp.where(
            jnp.logical_and(exists[side], tile_video[beside[side]] == own_video), 0.0, MASKED
        ).astype(jnp.float32)
        for side in (LEFT, RIGHT)
    ]

    if relays:

        @pl.when(passes)
        def _():
            pl.semaphore_wait(ready, 1)

    def attend(h, carry):
        pass_at(0, h)
        receive_at(0, h)

        @pl.when(h + early < heads)
        def _():
            start_sends(False)(h + early, 0)

        queries, grads = own[0, h], own[3, h]
        keys = (own[1, h], window[LEFT, 0, h], window[RIGHT, 0, h])
        values = (own[2, h], window[LEFT, 1, h], window[RIGHT, 1, h])
        scores = [matmul_nt(key, queries) * (scale * LOG2_E) for key in keys]
        scores = [scores[0], scores[1] + bias[LEFT], scores[2] + bias[RIGHT]]
        highest = functools.reduce(
            jnp.maximum, [jnp.max(s, axis=0, keepdims=True) for s in scores]
        )
        raised = [jnp.exp2(s - highest) for s in scores]
        row_total = sum(jnp.sum(r, axis=0, keepdims=True) for r in raised)
        inverse = 1.0 / row_total
        weights = [r * inverse for r in raised]
        rounded = [w.astype(jnp.bfloat16) for w in weights]
        grad_prob = [matmul_nt(value, grads) for value in values]
        row_delta = sum(
            jnp.sum(w * p, axis=0, keepdims=True) for w, p in zip(weights, grad_prob)
        )
        grad_score = [
            (w * (p - row_delta)).astype(jnp.bfloat16) for w, p in zip(weights, grad_prob)
        ]
        for place, side in ((1, LEFT), (2, RIGHT)):
            partial[side, 0, h] = (matmul_nn(grad_score[place], queries) * scale).astype(
                jnp.bfloat16
            )
            partial[side, 1, h] = matmul_nn(rounded[place], grads).astype(jnp.bfloat16)
            send(1, side, h)
        total[0, h] = matmul_nn(grad_score[0], queries) * scale
        total[1, h] = matmul_nn(rounded[0], grads)
        attended = sum(matmul_tn(v, r) for v, r in zip(values, rounded))
        grad_query = sum(matmul_tn(k, s) for k, s in zip(keys, grad_score)) * scale
        outputs[0][:, columns(h)] = attended.T.astype(jnp.bfloat16)
        outputs[1][:, columns(h)] = grad_query.T.astype(jnp.bfloat16)
        return carry

    lax.fori_loop(0, heads, attend, 0)

    def drain(phase):
        for side in (LEFT, RIGHT):
            sent(phase, side)
        passed(phase)

    drain(0)

    for batch, (first, _) in enumerate(passings[1]):
        if first < AHEAD:
            pass_on(1, batch)

    def finish(h, carry):
        pass_at(1, h + AHEAD)
        receive_at(1, h)
        for a in range(2):
            joined = (
                total[a, h]
                + returned[LEFT, a, h].astype(jnp.float32)
                + returned[RIGHT, a, h].astype(jnp.float32)
            )
            outputs[2 + a][:, columns(h)] = joined.astype(jnp.bfloat16)
        return carry

    lax.fori_loop(0, heads, finish, 0)

    drain(1)


def place_kernel(*refs):
    sources, targets, sem = refs[:4], refs[4:8], refs[8]
    copies = [
        pltpu.make_async_copy(source, target, sem.at[i])
        for i, (source, target) in enumerate(zip(sources, targets))
    ]
    for copy in copies:
        copy.start()
    for copy in copies:
        copy.wait()


def two_wide(mesh):
    spots = [
        (tuple(d.coords), d.core_on_chip) if hasattr(d, "coords") else None
        for d in mesh.devices.reshape(mesh.devices.shape[0], -1)[0]
    ]
    if len(spots) < 8 or len(spots) % 4 or None in spots:
        return False
    (x0, _, z0), _ = spots[0]
    return all(
        coords[0] - x0 == i // 2 % 2 and coords[2] - z0 == i // 4 and core == i % 2
        for i, (coords, core) in enumerate(spots)
    )


def solution(mesh):
    count = mesh.shape["frames"]
    relays = two_wide(mesh)

    def step(queries, keys, values, out_grad, tile_video):
        rows, width = queries.shape
        heads = width // HEAD_DIM
        tile = (heads, rows, HEAD_DIM)
        waits, passes = ([len(cut) for cut in cuts] for cuts in batches_of(heads))
        results = pl.pallas_call(
            functools.partial(kernel, count, heads, relays),
            out_shape=[jax.ShapeDtypeStruct((rows, width), jnp.bfloat16)] * 4,
            in_specs=[pl.BlockSpec(memory_space=pltpu.HBM)] * 5,
            out_specs=[pl.BlockSpec(memory_space=pltpu.VMEM)] * 4,
            scratch_shapes=[
                pltpu.VMEM((4,) + tile, jnp.bfloat16),
                pltpu.VMEM((2, 2) + tile, jnp.bfloat16),
                pltpu.VMEM((2, 2) + tile, jnp.bfloat16),
                pltpu.VMEM((2, 2) + tile, jnp.bfloat16),
                pltpu.VMEM((2,) + tile, jnp.float32),
                pltpu.VMEM((2, 2) + tile, jnp.bfloat16),
                pltpu.SMEM(tile_video.shape, tile_video.dtype),
                pltpu.SemaphoreType.DMA,
                pltpu.SemaphoreType.DMA,
                pltpu.SemaphoreType.DMA((2,)),
                pltpu.SemaphoreType.DMA((waits[0],)),
                pltpu.SemaphoreType.DMA((2,)),
                pltpu.SemaphoreType.DMA((waits[1],)),
                pltpu.SemaphoreType.DMA((2,)),
                pltpu.SemaphoreType.DMA((2, max(passes))),
                pltpu.SemaphoreType.DMA((3,)),
                pltpu.SemaphoreType.REGULAR,
            ],
            compiler_params=pltpu.CompilerParams(
                collective_id=0, has_side_effects=True, vmem_limit_bytes=49 * 1024 * 1024
            ),
        )(pltpu.with_memory_space_constraint(tile_video, pltpu.HBM), queries, keys, values, out_grad)
        return pl.pallas_call(
            place_kernel,
            out_shape=[jax.ShapeDtypeStruct((rows, width), jnp.bfloat16)] * 4,
            in_specs=[pl.BlockSpec(memory_space=pltpu.VMEM)] * 4,
            out_specs=[pl.BlockSpec(memory_space=pltpu.HBM)] * 4,
            scratch_shapes=[pltpu.SemaphoreType.DMA((4,))],
            compiler_params=pltpu.CompilerParams(vmem_limit_bytes=8 * 1024 * 1024),
        )(*results)

    rows = P(("groups", "frames"), None)
    return jax.shard_map(
        step,
        mesh=mesh,
        in_specs=(rows, rows, rows, rows, P("groups")),
        out_specs=(rows, rows, rows, rows),
        check_vma=False,
    )
```

```python
import functools

import jax
import jax.numpy as jnp
from jax import lax
from jax.experimental import pallas as pl
from jax.experimental.pallas import tpu as pltpu
from jax.sharding import PartitionSpec as P

HEAD_DIM = 128
MESH = pl.DeviceIdType.MESH
LEFT, RIGHT = 0, 1
LOG2_E = 1.4426950408889634
MASKED = -1e30
AHEAD = 3
BATCH = 3


def matmul_nt(a, b):
    return lax.dot_general(a, b, (((1,), (1,)), ((), ())), preferred_element_type=jnp.float32)


def matmul_tn(a, b):
    return lax.dot_general(a, b, (((0,), (0,)), ((), ())), preferred_element_type=jnp.float32)


def matmul_nn(a, b):
    return lax.dot_general(a, b, (((1,), (0,)), ((), ())), preferred_element_type=jnp.float32)


def batches_of(heads):
    even = range(0, heads, BATCH)
    arrivals = (even, sorted({0, heads // 2, heads * 3 // 4, heads - 1}))
    passes = (even, even)
    return [
        [
            [(first, last - first) for first, last in zip(firsts, list(firsts[1:]) + [heads])]
            for firsts in cut
        ]
        for cut in (arrivals, passes)
    ]


def kernel(
    count, heads, relays, video_hbm, q_hbm, k_hbm, v_hbm, g_hbm, o_ref, dq_ref, dk_ref, dv_ref,
    own, window, partial, returned, total, passing, tile_video, video_sem,
    own_sem, kv_send, kv_recv, ret_send, ret_recv, pass_send, pass_recv, part_sem, ready,
):
    group = lax.axis_index("groups")
    me = lax.axis_index("frames")
    exists = (me > 0, me < count - 1)
    beside = (jnp.maximum(me - 1, 0), jnp.minimum(me + 1, count - 1))
    scale = HEAD_DIM ** (-0.5)
    inputs = (q_hbm, k_hbm, v_hbm, g_hbm)
    outputs = (o_ref, dq_ref, dk_ref, dv_ref)

    def columns(h):
        return pl.ds(pl.multiple_of(h * HEAD_DIM, HEAD_DIM), HEAD_DIM)

    def load(a, h):
        return pltpu.make_async_copy(inputs[a].at[:, columns(h)], own.at[a, h], own_sem)

    place, plane, planes = lax.rem(me, 4), me // 4, count // 4
    batches, passings = batches_of(heads)
    up = jnp.logical_and(place % 2 == 1, plane < planes - 1)
    down = jnp.logical_and(place % 2 == 0, plane > 0)
    in_relay = jnp.logical_or(up, down)
    first_peer = jnp.where(in_relay, jnp.where(place < 2, me + 2, me - 2), 0)
    second_peer = jnp.where(in_relay, jnp.where(place % 2 == 1, me + 3, me - 3), 0)

    def share_of(lower, upward):
        return heads * ((planes - 1 - lower) if upward else (lower + 1)) // planes

    def picked(share, h):
        return (heads - h) * share // heads > (heads - 1 - h) * share // heads

    def rows_of(lower):
        return own.shape[2] * (lower + 3) // (planes + 2) // 16 * 16

    def batch_of(cut, h):
        return sum(jnp.where(h >= first, 1, 0) for first, _ in cut[1:])

    is_source = (jnp.logical_and(place == 0, plane > 0), jnp.logical_and(place == 3, up))
    passes_up = jnp.logical_and(place == 1, up)
    passes_down = jnp.logical_and(place == 2, down)

    lands = (window, returned)
    send_sems, recv_sems = (kv_send, ret_send), (kv_recv, ret_recv)

    def pieces(phase, side, h):
        if phase == 1:
            return [(partial.at[side, :, h], slice(None))]
        return [(inputs[1 + a].at[:, columns(h)], a) for a in range(2)]

    def direct_copies(phase, side, h):
        return [
            pltpu.make_async_remote_copy(
                src_ref=source,
                dst_ref=lands[phase].at[1 - side, a, h],
                send_sem=send_sems[phase].at[side],
                recv_sem=recv_sems[phase].at[batch_of(batches[phase], h)],
                device_id=(group, beside[side]),
                device_id_type=MESH,
            )
            for source, a in pieces(phase, side, h)
        ]

    def copies_to_relay(phase, side, h, most=2):
        return [
            pltpu.make_async_remote_copy(
                src_ref=source,
                dst_ref=passing.at[phase, a, h],
                send_sem=send_sems[phase].at[side],
                recv_sem=pass_recv.at[phase, batch_of(passings[phase], h)],
                device_id=(group, first_peer),
                device_id_type=MESH,
            )
            for source, a in pieces(phase, side, h)[:most]
        ]

    def copy_from_relay(phase, side, h):
        return pltpu.make_async_remote_copy(
            src_ref=passing.at[phase, :, h],
            dst_ref=lands[phase].at[side, :, h],
            send_sem=pass_send.at[phase],
            recv_sem=recv_sems[phase].at[batch_of(batches[phase], h)],
            device_id=(group, second_peer),
            device_id_type=MESH,
        )

    def values_to_relay(lower):
        near = pl.ds(0, rows_of(lower))
        far = pl.ds(rows_of(lower), own.shape[2] - rows_of(lower))
        return [
            pltpu.make_async_remote_copy(
                src_ref=inputs[2].at[near, columns(0)],
                dst_ref=passing.at[0, 1, 0, near],
                send_sem=kv_send.at[RIGHT],
                recv_sem=part_sem.at[0],
                device_id=(group, first_peer),
                device_id_type=MESH,
            ),
            pltpu.make_async_remote_copy(
                src_ref=inputs[2].at[far, columns(0)],
                dst_ref=window.at[LEFT, 1, 0, far],
                send_sem=kv_send.at[RIGHT],
                recv_sem=kv_recv.at[0],
                device_id=(group, beside[RIGHT]),
                device_id_type=MESH,
            ),
        ]

    def parts_from_relay(lower):
        near = pl.ds(0, rows_of(lower))
        return [
            pltpu.make_async_remote_copy(
                src_ref=source,
                dst_ref=target,
                send_sem=part_sem.at[1 + i],
                recv_sem=kv_recv.at[0],
                device_id=(group, second_peer),
                device_id_type=MESH,
            )
            for i, (source, target) in enumerate(
                [
                    (passing.at[0, 0, 0], window.at[LEFT, 0, 0]),
                    (passing.at[0, 1, 0, near], window.at[LEFT, 1, 0, near]),
                ]
            )
        ]

    def send(phase, side, h):
        lower = plane - 1 if side == LEFT else plane
        if relays:
            indirect = jnp.logical_and(is_source[side], picked(share_of(lower, side == RIGHT), h))
            direct = jnp.logical_and(exists[side], jnp.logical_not(indirect))

            parted = phase == 0 and side == RIGHT
            whole = jnp.logical_and(indirect, h > 0) if parted else indirect

            @pl.when(whole)
            def _():
                for copy in copies_to_relay(phase, side, h):
                    copy.start()

            for low in range(planes - 1 if parted else 0):

                @pl.when(jnp.logical_and(indirect, jnp.logical_and(h == 0, plane == low)))
                def _():
                    for copy in copies_to_relay(0, RIGHT, 0, 1) + values_to_relay(low):
                        copy.start()
        else:
            direct = exists[side]

        @pl.when(direct)
        def _():
            for copy in direct_copies(phase, side, h):
                copy.start()

    def arrived(buffer, sem):
        pltpu.make_async_copy(buffer, buffer, sem).wait()

    def receive(phase, batch):
        first, size = batches[phase][batch]
        for left in (True, False):
            for right in (True, False):
                if not (left or right):
                    continue
                sides = slice(None) if left and right else (LEFT if left else RIGHT)

                @pl.when(jnp.logical_and(exists[LEFT] == left, exists[RIGHT] == right))
                def _():
                    arrived(
                        lands[phase].at[sides, :, pl.ds(first, size)], recv_sems[phase].at[batch]
                    )

    def sent(phase, side):
        @pl.when(exists[side])
        def _():
            pltpu.make_async_remote_copy(
                src_ref=partial.at[side],
                dst_ref=lands[phase].at[1 - side],
                send_sem=send_sems[phase].at[side],
                recv_sem=recv_sems[phase].at[0],
                device_id=(group, beside[side]),
                device_id_type=MESH,
            ).wait_send()

    def passers():
        for lower in range(planes - 1 if relays else 0):
            yield lower, jnp.logical_and(passes_up, plane == lower), LEFT
            yield lower, jnp.logical_and(passes_down, plane == lower + 1), RIGHT

    def pass_on(phase, batch):
        first, size = passings[phase][batch]
        for lower, here, side in passers():
            share = share_of(lower, side == LEFT)
            through = [h for h in range(first, first + size) if picked(share, h)]
            if not through:
                continue
            parted = phase == 0 and side == LEFT and first == 0
            tiles = (0, pl.ds(0, 2 * len(through) - 1))
            due = tiles if parted else (slice(None), pl.ds(first, len(through)))

            @pl.when(here)
            def _():
                arrived(passing.at[(phase, *due)], pass_recv.at[phase, batch])
                if parted:
                    arrived(passing.at[0, 1, 0, pl.ds(0, rows_of(lower))], part_sem.at[0])
                    for copy in parts_from_relay(lower):
                        copy.start()
                for h in through[1:] if parted else through:
                    copy_from_relay(phase, side, h).start()

    def pass_at(phase, h):
        for batch, (first, _) in enumerate(passings[phase]):

            @pl.when(h == first)
            def _():
                pass_on(phase, batch)

    def receive_at(phase, h):
        for batch, (first, _) in enumerate(batches[phase]):

            @pl.when(h == first)
            def _():
                receive(phase, batch)

    def passed(phase):
        for lower, here, side in passers():
            parted = phase == 0 and side == LEFT
            share = share_of(lower, side == LEFT) - (1 if parted else 0)

            @pl.when(here)
            def _():
                if parted:
                    for copy in parts_from_relay(lower):
                        copy.wait_send()
                if share:
                    pltpu.make_async_remote_copy(
                        src_ref=passing.at[phase, :, pl.ds(0, share)],
                        dst_ref=lands[phase].at[side, :, pl.ds(0, share)],
                        send_sem=pass_send.at[phase],
                        recv_sem=recv_sems[phase].at[0],
                        device_id=(group, second_peer),
                        device_id_type=MESH,
                    ).wait_send()

    barrier = pltpu.get_barrier_semaphore()
    for side in (LEFT, RIGHT):

        @pl.when(exists[side])
        def _():
            pl.semaphore_signal(
                barrier, inc=1, device_id=(group, beside[side]), device_id_type=MESH
            )

    peers = jnp.minimum(me, 1) + jnp.minimum(count - 1 - me, 1)
    if relays:
        passes = jnp.logical_or(passes_up, passes_down)
        uses = jnp.logical_and(in_relay, jnp.logical_not(passes))

        @pl.when(passes)
        def _():
            for peer in (first_peer, second_peer):
                pl.semaphore_signal(barrier, inc=1, device_id=(group, peer), device_id_type=MESH)

        peers = peers + jnp.where(uses, 2, 0)
    pl.semaphore_wait(barrier, peers)

    def start_sends(crossing):
        def act(h, carry):
            for side in (LEFT, RIGHT):

                @pl.when((lax.rem(me, 2) == 1) == ((side == RIGHT) == crossing))
                def _():
                    send(0, side, h)

            return carry

        return act

    def start_loads(h, carry):
        for a in range(4):
            load(a, h).start()
        return carry

    early = min(AHEAD, heads)
    lax.fori_loop(0, heads, start_sends(True), 0)
    lax.fori_loop(0, early, start_sends(False), 0)
    if relays:

        @pl.when(uses)
        def _():
            pl.semaphore_signal(
                ready, inc=1, device_id=(group, second_peer), device_id_type=MESH
            )

    video_copy = pltpu.make_async_copy(video_hbm, tile_video, video_sem)
    video_copy.start()
    lax.fori_loop(0, heads, start_loads, 0)

    for side in (LEFT, RIGHT):

        @pl.when(jnp.logical_not(exists[side]))
        def _():
            def clear(h, carry):
                for a in range(2):
                    window[side, a, h] = jnp.zeros(window.shape[3:], window.dtype)
                    returned[side, a, h] = jnp.zeros(returned.shape[3:], returned.dtype)
                return carry

            lax.fori_loop(0, heads, clear, 0)

    video_copy.wait()
    arrived(own, own_sem)
    own_video = tile_video[me]
    bias = [
        jnp.where(
            jnp.logical_and(exists[side], tile_video[beside[side]] == own_video), 0.0, MASKED
        ).astype(jnp.float32)
        for side in (LEFT, RIGHT)
    ]

    if relays:

        @pl.when(passes)
        def _():
            pl.semaphore_wait(ready, 1)

    def attend(h, carry):
        pass_at(0, h)
        receive_at(0, h)

        @pl.when(h + early < heads)
        def _():
            start_sends(False)(h + early, 0)

        queries, grads = own[0, h], own[3, h]
        keys = (own[1, h], window[LEFT, 0, h], window[RIGHT, 0, h])
        values = (own[2, h], window[LEFT, 1, h], window[RIGHT, 1, h])
        scores = [matmul_nt(key, queries) * (scale * LOG2_E) for key in keys]
        scores = [scores[0], scores[1] + bias[LEFT], scores[2] + bias[RIGHT]]
        highest = functools.reduce(
            jnp.maximum, [jnp.max(s, axis=0, keepdims=True) for s in scores]
        )
        raised = [jnp.exp2(s - highest) for s in scores]
        row_total = sum(jnp.sum(r, axis=0, keepdims=True) for r in raised)
        inverse = 1.0 / row_total
        weights = [r * inverse for r in raised]
        rounded = [w.astype(jnp.bfloat16) for w in weights]
        grad_prob = [matmul_nt(value, grads) for value in values]
        row_delta = sum(
            jnp.sum(w * p, axis=0, keepdims=True) for w, p in zip(weights, grad_prob)
        )
        grad_score = [
            (w * (p - row_delta)).astype(jnp.bfloat16) for w, p in zip(weights, grad_prob)
        ]
        for place, side in ((1, LEFT), (2, RIGHT)):
            partial[side, 0, h] = (matmul_nn(grad_score[place], queries) * scale).astype(
                jnp.bfloat16
            )
            partial[side, 1, h] = matmul_nn(rounded[place], grads).astype(jnp.bfloat16)
            send(1, side, h)
        total[0, h] = matmul_nn(grad_score[0], queries) * scale
        total[1, h] = matmul_nn(rounded[0], grads)
        attended = sum(matmul_tn(v, r) for v, r in zip(values, rounded))
        grad_query = sum(matmul_tn(k, s) for k, s in zip(keys, grad_score)) * scale
        outputs[0][:, columns(h)] = attended.T.astype(jnp.bfloat16)
        outputs[1][:, columns(h)] = grad_query.T.astype(jnp.bfloat16)
        return carry

    lax.fori_loop(0, heads, attend, 0)

    def drain(phase):
        for side in (LEFT, RIGHT):
            sent(phase, side)
        passed(phase)

    drain(0)

    for batch, (first, _) in enumerate(passings[1]):
        if first < AHEAD:
            pass_on(1, batch)

    def finish(h, carry):
        pass_at(1, h + AHEAD)
        receive_at(1, h)
        for a in range(2):
            joined = (
                total[a, h]
                + returned[LEFT, a, h].astype(jnp.float32)
                + returned[RIGHT, a, h].astype(jnp.float32)
            )
            outputs[2 + a][:, columns(h)] = joined.astype(jnp.bfloat16)
        return carry

    lax.fori_loop(0, heads, finish, 0)

    drain(1)


def place_kernel(*refs):
    sources, targets, sem = refs[:4], refs[4:8], refs[8]
    copies = [
        pltpu.make_async_copy(source, target, sem.at[i])
        for i, (source, target) in enumerate(zip(sources, targets))
    ]
    for copy in copies:
        copy.start()
    for copy in copies:
        copy.wait()


def two_wide(mesh):
    spots = [
        (tuple(d.coords), d.core_on_chip) if hasattr(d, "coords") else None
        for d in mesh.devices.reshape(mesh.devices.shape[0], -1)[0]
    ]
    if len(spots) < 8 or len(spots) % 4 or None in spots:
        return False
    (x0, _, z0), _ = spots[0]
    return all(
        coords[0] - x0 == i // 2 % 2 and coords[2] - z0 == i // 4 and core == i % 2
        for i, (coords, core) in enumerate(spots)
    )


def solution(mesh):
    count = mesh.shape["frames"]
    relays = two_wide(mesh)

    def step(queries, keys, values, out_grad, tile_video):
        rows, width = queries.shape
        heads = width // HEAD_DIM
        tile = (heads, rows, HEAD_DIM)
        waits, passes = ([len(cut) for cut in cuts] for cuts in batches_of(heads))
        results = pl.pallas_call(
            functools.partial(kernel, count, heads, relays),
            out_shape=[jax.ShapeDtypeStruct((rows, width), jnp.bfloat16)] * 4,
            in_specs=[pl.BlockSpec(memory_space=pltpu.HBM)] * 5,
            out_specs=[pl.BlockSpec(memory_space=pltpu.VMEM)] * 4,
            scratch_shapes=[
                pltpu.VMEM((4,) + tile, jnp.bfloat16),
                pltpu.VMEM((2, 2) + tile, jnp.bfloat16),
                pltpu.VMEM((2, 2) + tile, jnp.bfloat16),
                pltpu.VMEM((2, 2) + tile, jnp.bfloat16),
                pltpu.VMEM((2,) + tile, jnp.float32),
                pltpu.VMEM((2, 2) + tile, jnp.bfloat16),
                pltpu.SMEM(tile_video.shape, tile_video.dtype),
                pltpu.SemaphoreType.DMA,
                pltpu.SemaphoreType.DMA,
                pltpu.SemaphoreType.DMA((2,)),
                pltpu.SemaphoreType.DMA((waits[0],)),
                pltpu.SemaphoreType.DMA((2,)),
                pltpu.SemaphoreType.DMA((waits[1],)),
                pltpu.SemaphoreType.DMA((2,)),
                pltpu.SemaphoreType.DMA((2, max(passes))),
                pltpu.SemaphoreType.DMA((3,)),
                pltpu.SemaphoreType.REGULAR,
            ],
            compiler_params=pltpu.CompilerParams(
                collective_id=0, has_side_effects=True, vmem_limit_bytes=49 * 1024 * 1024
            ),
        )(pltpu.with_memory_space_constraint(tile_video, pltpu.HBM), queries, keys, values, out_grad)
        return pl.pallas_call(
            place_kernel,
            out_shape=[jax.ShapeDtypeStruct((rows, width), jnp.bfloat16)] * 4,
            in_specs=[pl.BlockSpec(memory_space=pltpu.VMEM)] * 4,
            out_specs=[pl.BlockSpec(memory_space=pltpu.HBM)] * 4,
            scratch_shapes=[pltpu.SemaphoreType.DMA((4,))],
            compiler_params=pltpu.CompilerParams(vmem_limit_bytes=8 * 1024 * 1024),
        )(*results)

    rows = P(("groups", "frames"), None)
    return jax.shard_map(
        step,
        mesh=mesh,
        in_specs=(rows, rows, rows, rows, P("groups")),
        out_specs=(rows, rows, rows, rows),
        check_vma=False,
    )
```
